128 devices in a mesh: front: 8 (over y, core), blk: 16 (over z, x).
Axes of the slice: x: 4, y: 4, z: 4, core: 2. Of those that a mesh axis runs over, the one named last changes fastest.
Arguments:
- front: float32 [49152, 6144], P('front', 'blk'), may hold values from -8 to 96, as said below
- parent_group: int32 [8, 16, 6, 1], P('front', 'blk'), may hold values from 0 to 7; in each aligned block of 6 rows (0 to 5, 6 to 11, ..., all dimensions but the last counted through in order) at most 2 rows name the same one
- row_block: int32 [8, 16, 6], P('front', 'blk'), may hold values from 0 to 7
- parent_base: float32 [8192, 6144], P('front', 'blk'), may hold values from -6 to 6
Outputs:
- factored: float32 [49152, 6144], P('front', 'blk')
- assembled: float32 [8192, 6144], P('front', 'blk')
The draws below stay inside these ranges and needn't reach their ends.
Inputs may be any that keep to these rules, and one draw needn't show every extreme that they name: `parent_group`: in the 6 blocks of one device no group is named more than 2 times. `front`: diagonal entries at indices pivotal at some tick lie between 48 and 96; every other entry lies within 8 of zero.
All inputs are finite; a program needn't handle non-finite values.
Results may differ from the reference program's by a relative error of at most 0.003.
Values may be sent and summed in bfloat16 or wider, within the bound.
A program may use at most 128 MiB of HBM per device.

```python
import math
import jax
import jax.numpy as jnp
import numpy as np
from jax import lax

SLAB = 384
P_SIZE = 256
ROOT_P = 16
TICKS = 5
NEWTON = 2
RB = 128
NB = 6
CAP = 2
ASM_BLOCKS = 8
GROUPS = 8
SLABS = 16
F = 6144
ASM_ROWS = 1024


def draw_front(key, part):
    first, second = jax.random.split(jax.random.fold_in(key, 11))
    spread = jnp.clip(jax.random.normal(first, (GROUPS, F, F), jnp.float32), -6.0, 6.0)
    index = jnp.arange(F)
    pivotal = (index % SLAB < P_SIZE) & (index // SLAB < TICKS)
    factor = jnp.exp(jax.random.uniform(second, (GROUPS, F), jnp.float32, 0.0, math.log(2.0)))
    diagonal = 3.0 * ROOT_P * factor
    select = (index[:, None] == index[None, :]) & pivotal[None, :]
    matrix = jnp.where(select[None, :, :], diagonal[:, None, :], spread)
    return matrix.reshape(GROUPS * F, F).astype(jnp.float32)


def set_ends(array, own_key, low, largest):
    dims = array.shape
    spot = [jax.random.randint(jax.random.fold_in(own_key, axis), (), 0, dims[axis]) for axis in range(len(dims))]
    array = array.at[tuple(spot)].set(low)
    longest = dims.index(max(dims))
    spot[longest] = (spot[longest] + 1) % dims[longest]
    return array.at[tuple(spot)].set(largest)


def block_scale(stream_key, shape, cuts, smallest, largest):
    loudness, own = 1.0, jax.random.fold_in(stream_key, 6)
    for position, shards_of in cuts:
        draws = jnp.exp(jax.random.uniform(jax.random.fold_in(own, position), (shards_of,), jnp.float32, smallest / len(cuts), largest / len(cuts)))
        loudness = loudness * jnp.repeat(draws, shape[position] // shards_of).reshape([-1 if axis == position else 1 for axis in range(len(shape))])
    return loudness


def routed_block(own_key, own, number, rows, number_of, top, most, skew):
    sequence = jax.random.permutation(own_key, number_of)
    crowded, common = portions_of(number_of, rows * top, most, skew, True), portions_of(number_of, rows * top, most, skew, False)
    places = jnp.arange(number_of)

    def named(tallies, offset_by):
        used = int((tallies > 0).sum())
        fixed = max(1, used // 4)
        passed = fixed + (places - fixed + offset_by * (used - fixed)) % max(1, number_of - fixed)
        return jnp.zeros((number_of,), jnp.int32).at[sequence[jnp.where(places < fixed, places, passed)]].set(jnp.asarray(tallies, jnp.int32))

    tallies = jnp.where(number % 4 == 0, named(crowded, number // 4), named(common, number - number // 4 - 1))
    mixed = jax.random.permutation(jax.random.fold_in(own, 3), number_of)
    donor, sink = mixed[0:number_of // 2 * 2:2], mixed[1:number_of // 2 * 2:2]
    room = jnp.minimum(tallies[donor] - 1, most - tallies[sink]) // 2
    room = jnp.where((donor == sequence[0]) | (sink == sequence[0]) | (tallies[sink] == 0), 0, jnp.maximum(room, 0))
    passed = jax.random.randint(jax.random.fold_in(own, 4), (number_of // 2,), 0, 1 << 20) % (room + 1)
    tallies = tallies.at[donor].add(-passed).at[sink].add(passed)
    members = jnp.searchsorted(jnp.cumsum(tallies), jnp.arange(rows * top), side="right").astype(jnp.int32)
    listing = members.reshape(top, rows).T
    listing = listing[jax.random.permutation(jax.random.fold_in(own, 1), rows)]
    offset_by = jax.random.randint(jax.random.fold_in(own, 2), (rows, 1), 0, top)
    return jnp.take_along_axis(listing, (jnp.arange(top)[None, :] + offset_by) % top, axis=1)


def portions_of(count, total, limit, lean, full):
    weights = [(1 << 20) // math.isqrt(standing ** lean) + 1 for standing in range(1, count + 1)]
    largest = limit if full else min(limit, max(-(-total // count), total * weights[0] // sum(weights)))
    least = 1 if total - largest >= count - 1 else 0
    holding, spare = [largest] + [least] * (count - 1), total - largest - least * (count - 1)
    while spare > 0:
        free = [i for i in range(1, count) if holding[i] < largest] or [i for i in range(1, count) if holding[i] < limit]
        pool, remaining = sum([weights[i] for i in free]), spare
        for i in free:
            more = min(limit - holding[i], max(1, remaining * weights[i] // pool), spare)
            holding[i] = holding[i] + more
            spare = spare - more
    return np.array(holding)


def noise(key, shape, deviation, most, shards=(), kind=jnp.bfloat16):
    result = deviation * jax.random.normal(key, shape, jnp.float32)
    if shards:
        result = result * block_scale(key, shape, shards, -0.22, 0.18)
    return jnp.clip(result, -most, most).astype(kind)


def setup_inputs(seed: int = 0) -> dict:
    key_list = jax.random.split(jax.random.key(seed), 5)
    front = draw_front(jax.random.fold_in(key_list[4], 71), 0)
    parent_group_keys = jax.random.split(jax.random.fold_in(key_list[1], 1), GROUPS * SLABS * NB // NB)
    parent_group_turns = jax.random.permutation(jax.random.fold_in(key_list[1], 3), GROUPS * SLABS * NB // NB)
    parent_group = jax.vmap(lambda own, number: routed_block(jax.random.fold_in(key_list[1], 2), own, number, NB, GROUPS, 1, CAP, 2))(parent_group_keys, parent_group_turns).reshape((GROUPS, SLABS, NB, 1))
    row_block = set_ends(jax.random.randint(key_list[2], (GROUPS, SLABS, NB), 0, ASM_BLOCKS), jax.random.fold_in(key_list[2], 1), 0, ASM_BLOCKS - 1).astype(jnp.int32)
    parent_base = noise(key_list[3], (GROUPS * ASM_ROWS, F), 1.0, 6.0, ((0, 8), (1, 16)), jnp.float32)
    return {"front": front, "parent_group": parent_group, "row_block": row_block, "parent_base": parent_base}


def newton_inverse(block):
    inverse = jnp.diag(1.0 / jnp.diagonal(block))
    ident = jnp.eye(block.shape[0], dtype=block.dtype)
    for step in range(NEWTON):
        inverse = jnp.dot(inverse, 2.0 * ident - jnp.dot(block, inverse, precision=lax.Precision.HIGHEST), precision=lax.Precision.HIGHEST)
    return inverse


def factor_front(matrix):
    order = matrix.shape[0]
    index = jnp.arange(order)
    pivotal = index % SLAB < P_SIZE
    for tick in range(TICKS):
        start = tick * SLAB
        live = jnp.logical_not(pivotal & (index // SLAB <= tick))
        inverse = newton_inverse(matrix[start:start + P_SIZE, start:start + P_SIZE])
        mult = jnp.dot(matrix[:, start:start + P_SIZE], inverse, precision=lax.Precision.HIGHEST)
        mult = mult * live[:, None].astype(matrix.dtype)
        panel = mult.astype(jnp.bfloat16)
        urows = matrix[start:start + P_SIZE, :].astype(jnp.bfloat16)
        change = jnp.dot(panel, urows, preferred_element_type=jnp.float32)
        matrix = matrix - change * live[None, :].astype(matrix.dtype)
        matrix = matrix.at[:, start:start + P_SIZE].set(jnp.where(live[:, None], mult, matrix[:, start:start + P_SIZE]))
    return matrix


def reference(front, parent_group, row_block, parent_base):
    fronts = front.reshape(GROUPS, F, F)
    factored = lax.map(factor_front, fronts)
    index = jnp.arange(F)
    keep = jnp.logical_not((index % SLAB < P_SIZE) & (index // SLAB < TICKS))
    tail = factored[:, F - NB * RB:, :] * keep[None, None, :].astype(factored.dtype)
    cont = lax.optimization_barrier(tail.astype(jnp.bfloat16)).astype(jnp.float32)
    cont = cont.reshape(GROUPS, NB, RB, SLABS, SLAB)
    dest = parent_group[..., 0]
    to_group = dest[..., None] == jnp.arange(GROUPS, dtype=jnp.int32)
    to_block = row_block[..., None] == jnp.arange(ASM_BLOCKS, dtype=jnp.int32)
    route = (to_group[..., :, None] & to_block[..., None, :]).astype(jnp.float32)
    added = jnp.einsum("gbipo,girbc->porbc", route, cont)
    base = parent_base.reshape(GROUPS, ASM_BLOCKS, RB, SLABS, SLAB)
    assembled = (base + added).reshape(GROUPS * ASM_ROWS, F)
    return factored.reshape(GROUPS * F, F), assembled
```

```python
import jax
import jax.numpy as jnp
from jax import lax
from jax.experimental import pallas as pl
from jax.experimental.pallas import tpu as pltpu
from jax.sharding import PartitionSpec as P

P_SIZE = 256
TICKS = 5
RB = 128
NB = 6
CAP = 2
ASM_BLOCKS = 8
SIDE = 4
WIDTH = 384
BLOCK = 256
HALF = BLOCK // 2
BLOCKS = 24
F32 = jnp.float32
BF16 = jnp.bfloat16

STEPS = ((1, 0), (0, 1), (-1, 0), (0, -1))
PARENT = {
    (1, 0): 0, (2, 0): 0, (3, 0): 0, (0, 1): 2, (1, 1): 1, (2, 1): 0, (3, 1): 0, (0, 2): 2,
    (1, 2): 1, (2, 2): 1, (3, 2): 0, (0, 3): 2, (1, 3): 3, (2, 3): 3, (3, 3): 0,
}
SENDERS = tuple(
    sorted(
        ((x - STEPS[way][0]) % SIDE) + SIDE * ((z - STEPS[way][1]) % SIDE)
        for (x, z), own in PARENT.items()
        if own == way
    )
    for way in range(4)
)


def pieces(block):
    if block < TICKS:
        return ((block * WIDTH, BLOCK),)
    if block < 8:
        return ((5376 + (block - TICKS) * BLOCK, BLOCK),)
    if block < 10:
        first = (block - 8) * 2 * WIDTH + P_SIZE
        return ((first, HALF), (first + WIDTH, HALF))
    return ((1792 + (block - 10) * BLOCK, BLOCK),)


def split(value):
    high = value.astype(BF16)
    return high, (value - high.astype(F32)).astype(BF16)


def dot(a, b):
    return jnp.dot(a, b, preferred_element_type=F32)


def dot3(a, b):
    return dot(a[0], b[0]) + dot(a[0], b[1]) + dot(a[1], b[0])


def kernel(front, out, rows, panel, urows, inv_high, inv_low, load_sem, store_sem, send_sem, recv_sem):
    me = lax.axis_index("blk")
    x = lax.rem(me, SIDE)
    z = lax.div(me, SIDE)
    around = [
        z * SIDE + lax.rem(x + 1, SIDE),
        lax.rem(z + 1, SIDE) * SIDE + x,
        z * SIDE + lax.rem(x + SIDE - 1, SIDE),
        lax.rem(z + SIDE - 1, SIDE) * SIDE + x,
    ]

    for block in range(BLOCKS):
        at = 0
        for start, size in pieces(block):
            pltpu.make_async_copy(
                front.at[pl.ds(start, size)], rows.at[block, pl.ds(at, size)], load_sem.at[block]
            ).start()
            at += size

    barrier = pltpu.get_barrier_semaphore()
    for other in around:
        pl.semaphore_signal(barrier, inc=1, device_id={"blk": other}, device_id_type=pl.DeviceIdType.MESH)
    pl.semaphore_wait(barrier, 4)

    def children(tick):
        dx = lax.rem(x - tick % SIDE + SIDE, SIDE)
        dz = lax.rem(z - tick // SIDE + SIDE, SIDE)
        nx, nz = lax.rem(SIDE - dx, SIDE), lax.rem(SIDE - dz, SIDE)
        turned = (dx + SIDE * dz, dz + SIDE * nx, nx + SIDE * nz, nz + SIDE * dx)
        result = []
        for tree in range(4):
            ways = []
            for way in range(4):
                has = turned[tree] == SENDERS[(way - tree) % 4][0]
                for node in SENDERS[(way - tree) % 4][1:]:
                    has = has | (turned[tree] == node)
                ways.append(has)
            result.append(ways)
        return result

    sends = [children(tick) for tick in range(TICKS)]

    def chunk_copy(tick, block, half, way):
        chunk = panel.at[tick, block, pl.ds(half * HALF, HALF)]
        return pltpu.make_async_remote_copy(
            src_ref=chunk,
            dst_ref=chunk,
            send_sem=send_sem.at[tick, way],
            recv_sem=recv_sem.at[tick, block, half],
            device_id={"blk": around[way]},
            device_id_type=pl.DeviceIdType.MESH,
        )

    def send(tick, block, pair):
        for half in range(2):
            tree = pair * 2 + half
            for way in range(4):
                @pl.when(sends[tick][tree][way])
                def _():
                    chunk_copy(tick, block, half, way).start()

    def receive(tick, block, pair):
        for half in range(2):
            tree = pair * 2 + half
            chunk_copy(tick, block, half, 0).wait_recv()
            for way in range(4):
                @pl.when(sends[tick][tree][way])
                def _():
                    chunk_copy(tick, block, half, way).start()

    def wait_load(block):
        pltpu.make_async_copy(front.at[pl.ds(0, BLOCK)], rows.at[block], load_sem.at[block]).wait()

    def store(block):
        return pltpu.make_async_copy(rows.at[block], out.at[block], store_sem.at[block])

    def invert(tick):
        matrix = rows[tick, :, :P_SIZE]
        line = lax.broadcasted_iota(jnp.int32, (P_SIZE, P_SIZE), 0)
        column = lax.broadcasted_iota(jnp.int32, (P_SIZE, P_SIZE), 1)
        eye = line == column
        on_diagonal = jnp.where(eye, matrix, 0.0)
        by_row = 1.0 / jnp.sum(on_diagonal, axis=1, keepdims=True)
        by_column = 1.0 / jnp.sum(on_diagonal, axis=0, keepdims=True)
        first = jnp.where(eye, 2.0 * by_row, 0.0) - by_row * matrix * by_column
        first = split(first)
        residual = jnp.where(eye, 2.0, 0.0) - dot3(split(matrix), first)
        high, low = split(dot3(first, split(residual)))
        inv_high[...] = high
        inv_low[...] = low

    def multiply(tick, block):
        mult = dot3(split(rows[block, :, :P_SIZE]), (inv_high[...], inv_low[...]))
        rows[block, :, :P_SIZE] = mult
        panel[tick, block] = mult.astype(BF16)

    def pivot_rows(tick):
        keep = jnp.where(me > tick, 1.0, 0.0).astype(F32)
        urows[:, :P_SIZE] = (rows[tick, :, :P_SIZE] * keep).astype(BF16)
        urows[:, P_SIZE:] = rows[tick, :, P_SIZE:].astype(BF16)

    def paired(first, body):
        body(first, 0)
        count = BLOCKS - 1 - first

        def step(index, carry):
            body(first + 1 + 2 * index, 1)
            body(first + 2 + 2 * index, 0)
            return carry

        lax.fori_loop(0, count // 2, step, 0)
        if count % 2:
            body(BLOCKS - 1, 1)

    wait_load(0)
    store(0).start()

    @pl.when(me == 0)
    def _():
        invert(0)

        def own(block, pair):
            wait_load(block)
            multiply(0, block)
            send(0, block, pair)

        paired(1, own)

    for tick in range(TICKS):
        pivot_rows(tick)

        def visit(block, pair):
            @pl.when(me != tick)
            def _():
                receive(tick, block, pair)
                if tick == 0:
                    wait_load(block)

            rows[block] = rows[block] - dot(panel[tick, block], urows[...])
            if tick + 1 < TICKS:
                is_pivot = isinstance(block, int) and block == tick + 1
                if is_pivot:
                    store(block).start()

                @pl.when(me == tick + 1)
                def _():
                    if is_pivot:
                        invert(tick + 1)
                    else:
                        multiply(tick + 1, block)
                        send(tick + 1, block, 1 - pair)
            else:
                store(block).start()

        paired(tick + 1, visit)

    for tick in range(TICKS):
        number = BLOCKS - 1 - tick
        for pair, amount in enumerate((number - number // 2, number // 2)):
            for way in range(4):
                @pl.when(sends[tick][2 * pair][way] | sends[tick][2 * pair + 1][way])
                def _():
                    sent = panel.at[tick, pl.ds(0, amount), pl.ds(0, HALF)]
                    pltpu.make_async_remote_copy(
                        src_ref=sent,
                        dst_ref=sent,
                        send_sem=send_sem.at[tick, way],
                        recv_sem=recv_sem.at[tick, 0, 0],
                        device_id={"blk": around[way]},
                        device_id_type=pl.DeviceIdType.MESH,
                    ).wait_send()
    for block in range(BLOCKS):
        store(block).wait()


def factor(front):
    return pl.pallas_call(
        kernel,
        out_shape=jax.ShapeDtypeStruct((BLOCKS, BLOCK, WIDTH), F32),
        in_specs=[pl.BlockSpec(memory_space=pl.ANY)],
        out_specs=pl.BlockSpec(memory_space=pl.ANY),
        scratch_shapes=[
            pltpu.VMEM((BLOCKS, BLOCK, WIDTH), F32),
            pltpu.VMEM((TICKS, BLOCKS, BLOCK, P_SIZE), BF16),
            pltpu.VMEM((P_SIZE, WIDTH), BF16),
            pltpu.VMEM((P_SIZE, P_SIZE), BF16),
            pltpu.VMEM((P_SIZE, P_SIZE), BF16),
            pltpu.SemaphoreType.DMA((BLOCKS,)),
            pltpu.SemaphoreType.DMA((BLOCKS,)),
            pltpu.SemaphoreType.DMA((TICKS, 4)),
            pltpu.SemaphoreType.DMA((TICKS, BLOCKS, 2)),
        ],
        compiler_params=pltpu.CompilerParams(
            collective_id=0, has_side_effects=True, vmem_limit_bytes=50 * 1024 * 1024
        ),
        name="factor",
    )(front)


def local(front, parent_group, row_block, parent_base):
    order, width = front.shape
    member = lax.axis_index("blk")
    groups = lax.axis_size("front")
    held = factor(front)
    parts = []
    for block in range(BLOCKS):
        at = 0
        for start, size in pieces(block):
            parts.append((start, held[block, at : at + size]))
            at += size
    parts.sort(key=lambda part: part[0])
    factored = jnp.concatenate([part[1] for part in parts], axis=0)

    keep_left = (member >= TICKS).astype(F32)
    tail = held[TICKS : TICKS + 3].reshape(NB * RB, width)
    tail = jnp.concatenate([tail[:, :P_SIZE] * keep_left, tail[:, P_SIZE:]], axis=1)
    cont = tail.astype(BF16).reshape(NB, RB, width)
    dest = parent_group.reshape(NB)
    target_block = row_block.reshape(NB)
    offset_hot = (target_block[:, None] == jnp.arange(ASM_BLOCKS, dtype=jnp.int32)[None, :]).astype(BF16)
    number = jnp.arange(NB)
    earlier = (dest[None, :] == dest[:, None]) & (number[None, :] < number[:, None])
    slot = jnp.sum(earlier.astype(jnp.int32), axis=1)
    pick = (dest[None, None, :] == jnp.arange(groups, dtype=jnp.int32)[:, None, None]) & (
        slot[None, None, :] == jnp.arange(CAP, dtype=jnp.int32)[None, :, None]
    )
    pick = pick.astype(BF16)
    outgoing = jnp.einsum("gci,irk->gcrk", pick, cont, preferred_element_type=F32).astype(BF16)
    address = jnp.einsum("gci,ia->gca", pick, offset_hot, preferred_element_type=F32).astype(BF16)
    incoming, received_address = (
        lax.all_to_all(outgoing, "front", split_axis=0, concat_axis=0, tiled=True),
        lax.all_to_all(address, "front", split_axis=0, concat_axis=0, tiled=True),
    )
    added = jnp.einsum("gca,gcrk->ark", received_address, incoming, preferred_element_type=F32)
    assembled = parent_base + added.reshape(ASM_BLOCKS * RB, width)
    return (factored, assembled)


def solution(mesh):
    placed = (
        P("front", "blk"),
        P("front", "blk", None, None),
        P("front", "blk", None),
        P("front", "blk"),
    )
    return jax.shard_map(
        local,
        mesh=mesh,
        in_specs=placed,
        out_specs=(P("front", "blk"), P("front", "blk")),
        check_vma=False,
    )
```

```python
import jax
import jax.numpy as jnp
from jax import lax
from jax.experimental import pallas as pl
from jax.experimental.pallas import tpu as pltpu
from jax.sharding import PartitionSpec as P

P_SIZE = 256
TICKS = 5
RB = 128
NB = 6
CAP = 2
ASM_BLOCKS = 8
SIDE = 4
WIDTH = 384
BLOCK = 256
HALF = BLOCK // 2
CHUNK = BLOCK // 4
LAG = 3
BEHIND = 5 * LAG
BLOCKS = 24
F32 = jnp.float32
BF16 = jnp.bfloat16

STEPS = ((1, 0), (0, 1), (-1, 0), (0, -1))
PARENT = {
    (1, 0): 0, (2, 0): 0, (3, 0): 0, (0, 1): 2, (1, 1): 1, (2, 1): 0, (3, 1): 0, (0, 2): 2,
    (1, 2): 1, (2, 2): 1, (3, 2): 0, (0, 3): 2, (1, 3): 3, (2, 3): 3, (3, 3): 0,
}
SENDERS = tuple(
    sorted(
        ((x - STEPS[way][0]) % SIDE) + SIDE * ((z - STEPS[way][1]) % SIDE)
        for (x, z), own in PARENT.items()
        if own == way
    )
    for way in range(4)
)


def depth_of(node):
    depth = 0
    while node != (0, 0):
        step = STEPS[PARENT[node]]
        node = ((node[0] - step[0]) % SIDE, (node[1] - step[1]) % SIDE)
        depth += 1
    return depth


DEPTH = {x + SIDE * z: depth_of((x, z)) for x, z in PARENT}


def pieces(block):
    if block < TICKS:
        return ((block * WIDTH, BLOCK),)
    if block < 8:
        return ((5376 + (block - TICKS) * BLOCK, BLOCK),)
    if block < 10:
        first = (block - 8) * 2 * WIDTH + P_SIZE
        return ((first, HALF), (first + WIDTH, HALF))
    return ((1792 + (block - 10) * BLOCK, BLOCK),)


def number(tick):
    return BLOCKS - 1 - tick


def split(value):
    high = value.astype(BF16)
    return high, (value - high.astype(F32)).astype(BF16)


def dot(a, b):
    return jnp.dot(a, b, preferred_element_type=F32)


def dot3(a, b):
    return dot(a[0], b[0]) + dot(a[0], b[1]) + dot(a[1], b[0])


def kernel(front, out, rows, panel, urows, inv_high, inv_low, load_sem, store_sem, send_sem, recv_sem):
    me = lax.axis_index("blk")
    x = lax.rem(me, SIDE)
    z = lax.div(me, SIDE)
    around = [
        z * SIDE + lax.rem(x + 1, SIDE),
        lax.rem(z + 1, SIDE) * SIDE + x,
        z * SIDE + lax.rem(x + SIDE - 1, SIDE),
        lax.rem(z + SIDE - 1, SIDE) * SIDE + x,
    ]

    for block in range(BLOCKS):
        at = 0
        for start, size in pieces(block):
            pltpu.make_async_copy(
                front.at[pl.ds(start, size)], rows.at[block, pl.ds(at, size)], load_sem.at[block]
            ).start()
            at += size

    barrier = pltpu.get_barrier_semaphore()
    for other in around:
        pl.semaphore_signal(barrier, inc=1, device_id={"blk": other}, device_id_type=pl.DeviceIdType.MESH)
    pl.semaphore_wait(barrier, 4)

    def place(tick):
        dx = lax.rem(x - tick % SIDE + SIDE, SIDE)
        dz = lax.rem(z - tick // SIDE + SIDE, SIDE)
        nx, nz = lax.rem(SIDE - dx, SIDE), lax.rem(SIDE - dz, SIDE)
        turned = (dx + SIDE * dz, dz + SIDE * nx, nx + SIDE * nz, nz + SIDE * dx)
        result = []
        lags = []
        for tree in range(4):
            ways = []
            for way in range(4):
                has = turned[tree] == SENDERS[(way - tree) % 4][0]
                for node in SENDERS[(way - tree) % 4][1:]:
                    has = has | (turned[tree] == node)
                ways.append(has)
            result.append(ways)
            lag = jnp.int32(0)
            for node, depth in DEPTH.items():
                lag = jnp.where(turned[tree] == node, depth * LAG, lag)
            lags.append(lag)
        return result, lags

    places = [place(tick) for tick in range(TICKS)]

    def chunk_copy(tick, block, tree, way):
        chunk = panel.at[tick, block, pl.ds(tree * CHUNK, CHUNK)]
        return pltpu.make_async_remote_copy(
            src_ref=chunk,
            dst_ref=chunk,
            send_sem=send_sem.at[tick, way],
            recv_sem=recv_sem.at[tick, block, tree],
            device_id={"blk": around[way]},
            device_id_type=pl.DeviceIdType.MESH,
        )

    def send(tick, block, tree):
        for way in range(4):
            @pl.when(places[tick][0][tree][way])
            def _():
                chunk_copy(tick, block, tree, way).start()

    def forward(tick, slot):
        for tree in range(4):
            index = slot - places[tick][1][tree]

            @pl.when((me != tick) & (index >= 0) & (index < number(tick)))
            def _():
                block = tick + 1 + index
                chunk_copy(tick, block, tree, 0).wait_recv()
                send(tick, block, tree)

    def wait_load(block):
        pltpu.make_async_copy(front.at[pl.ds(0, BLOCK)], rows.at[block], load_sem.at[block]).wait()

    def store(block):
        for half in range(2):
            part = block * 2 + half
            if isinstance(block, int) and block < TICKS:
                start = block * WIDTH + half * HALF
            else:
                start = jnp.where(
                    part < 16, 4096 + part * HALF, jnp.where(part < 20, (part - 16) * WIDTH + P_SIZE, part * HALF - 768)
                )
                start = pl.multiple_of(start, HALF)
            pltpu.make_async_copy(
                rows.at[block, pl.ds(half * HALF, HALF)], out.at[pl.ds(start, HALF)], store_sem.at[block]
            ).start()

    def invert(tick):
        matrix = rows[tick, :, :P_SIZE]
        line = lax.broadcasted_iota(jnp.int32, (P_SIZE, P_SIZE), 0)
        column = lax.broadcasted_iota(jnp.int32, (P_SIZE, P_SIZE), 1)
        eye = line == column
        on_diagonal = jnp.where(eye, matrix, 0.0)
        by_row = 1.0 / jnp.sum(on_diagonal, axis=1, keepdims=True)
        by_column = 1.0 / jnp.sum(on_diagonal, axis=0, keepdims=True)
        first = jnp.where(eye, 2.0 * by_row, 0.0) - by_row * matrix * by_column
        first = split(first)
        residual = jnp.where(eye, 2.0, 0.0) - dot3(split(matrix), first)
        high, low = split(dot3(first, split(residual)))
        inv_high[...] = high
        inv_low[...] = low

    def multiply(tick, block):
        mult = dot3(split(rows[block, :, :P_SIZE]), (inv_high[...], inv_low[...]))
        rows[block, :, :P_SIZE] = mult
        panel[tick, block] = mult.astype(BF16)

    def pivot_rows(tick):
        keep = jnp.where(me > tick, 1.0, 0.0).astype(F32)
        urows[:, :P_SIZE] = (rows[tick, :, :P_SIZE] * keep).astype(BF16)
        urows[:, P_SIZE:] = rows[tick, :, P_SIZE:].astype(BF16)

    def loop(first, last, body):
        def step(index, carry):
            body(index)
            return carry

        lax.fori_loop(first, last, step, 0)

    wait_load(0)
    store(0)

    @pl.when(me == 0)
    def _():
        invert(0)

        def own(block):
            wait_load(block)
            multiply(0, block)
            for tree in range(4):
                send(0, block, tree)

        loop(1, BLOCKS, own)

    def update(tick, block, pivot=False):
        if tick == 0:
            @pl.when(me != 0)
            def _():
                wait_load(block)

        rows[block] = rows[block] - dot(panel[tick, block], urows[...])
        if pivot or tick == TICKS - 1:
            store(block)
        if tick + 1 < TICKS:
            @pl.when(me == tick + 1)
            def _():
                if pivot:
                    invert(tick + 1)
                else:
                    multiply(tick + 1, block)
                    for tree in range(4):
                        send(tick + 1, block, tree)

    for tick in range(TICKS + 1):
        def early(slot):
            if tick > 0:
                forward(tick - 1, number(tick - 1) + slot)
            if tick < TICKS:
                forward(tick, slot)
            if tick > 0:
                update(tick - 1, tick + number(tick - 1) - BEHIND + slot)

        loop(0, BEHIND, early)
        if tick < TICKS:
            pivot_rows(tick)
            forward(tick, BEHIND)
            update(tick, tick + 1, pivot=tick + 1 < TICKS)

            def late(slot):
                forward(tick, slot)
                update(tick, tick + 1 - BEHIND + slot)

            loop(BEHIND + 1, number(tick), late)

    for tick in range(TICKS):
        for way in range(4):
            used = places[tick][0][0][way]
            for tree in range(1, 4):
                used = used | places[tick][0][tree][way]

            @pl.when(used)
            def _():
                sent = panel.at[tick, pl.ds(0, number(tick)), pl.ds(0, CHUNK)]
                pltpu.make_async_remote_copy(
                    src_ref=sent,
                    dst_ref=sent,
                    send_sem=send_sem.at[tick, way],
                    recv_sem=recv_sem.at[tick, 0, 0],
                    device_id={"blk": around[way]},
                    device_id_type=pl.DeviceIdType.MESH,
                ).wait_send()
    for block in range(BLOCKS):
        pltpu.make_async_copy(rows.at[block], out.at[pl.ds(0, BLOCK)], store_sem.at[block]).wait()


def factor(front):
    return pl.pallas_call(
        kernel,
        out_shape=jax.ShapeDtypeStruct(front.shape, F32),
        in_specs=[pl.BlockSpec(memory_space=pl.ANY)],
        out_specs=pl.BlockSpec(memory_space=pl.ANY),
        scratch_shapes=[
            pltpu.VMEM((BLOCKS, BLOCK, WIDTH), F32),
            pltpu.VMEM((TICKS, BLOCKS, BLOCK, P_SIZE), BF16),
            pltpu.VMEM((P_SIZE, WIDTH), BF16),
            pltpu.VMEM((P_SIZE, P_SIZE), BF16),
            pltpu.VMEM((P_SIZE, P_SIZE), BF16),
            pltpu.SemaphoreType.DMA((BLOCKS,)),
            pltpu.SemaphoreType.DMA((BLOCKS,)),
            pltpu.SemaphoreType.DMA((TICKS, 4)),
            pltpu.SemaphoreType.DMA((TICKS, BLOCKS, 4)),
        ],
        compiler_params=pltpu.CompilerParams(
            collective_id=0, has_side_effects=True, vmem_limit_bytes=50 * 1024 * 1024
        ),
        name="factor",
    )(front)


def local(front, parent_group, row_block, parent_base):
    order, width = front.shape
    member = lax.axis_index("blk")
    groups = lax.axis_size("front")
    factored = factor(front)
    keep_left = (member >= TICKS).astype(F32)
    tail = factored[order - NB * RB :]
    tail = jnp.concatenate([tail[:, :P_SIZE] * keep_left, tail[:, P_SIZE:]], axis=1)
    cont = tail.astype(BF16).reshape(NB, RB, width)
    dest = parent_group.reshape(NB)
    target_block = row_block.reshape(NB)
    offset_hot = (target_block[:, None] == jnp.arange(ASM_BLOCKS, dtype=jnp.int32)[None, :]).astype(BF16)
    number = jnp.arange(NB)
    earlier = (dest[None, :] == dest[:, None]) & (number[None, :] < number[:, None])
    slot = jnp.sum(earlier.astype(jnp.int32), axis=1)
    pick = (dest[None, None, :] == jnp.arange(groups, dtype=jnp.int32)[:, None, None]) & (
        slot[None, None, :] == jnp.arange(CAP, dtype=jnp.int32)[None, :, None]
    )
    pick = pick.astype(BF16)
    outgoing = jnp.einsum("gci,irk->gcrk", pick, cont, preferred_element_type=F32).astype(BF16)
    address = jnp.einsum("gci,ia->gca", pick, offset_hot, preferred_element_type=F32).astype(BF16)
    incoming, received_address = (
        lax.all_to_all(outgoing, "front", split_axis=0, concat_axis=0, tiled=True),
        lax.all_to_all(address, "front", split_axis=0, concat_axis=0, tiled=True),
    )
    added = jnp.einsum("gca,gcrk->ark", received_address, incoming, preferred_element_type=F32)
    assembled = parent_base + added.reshape(ASM_BLOCKS * RB, width)
    return (factored, assembled)


def solution(mesh):
    placed = (
        P("front", "blk"),
        P("front", "blk", None, None),
        P("front", "blk", None),
        P("front", "blk"),
    )
    return jax.shard_map(
        local,
        mesh=mesh,
        in_specs=placed,
        out_specs=(P("front", "blk"), P("front", "blk")),
        check_vma=False,
    )
```

```python
import jax
import jax.numpy as jnp
from jax import lax
from jax.experimental import pallas as pl
from jax.experimental.pallas import tpu as pltpu
from jax.sharding import PartitionSpec as P

P_SIZE = 256
TICKS = 5
RB = 128
NB = 6
CAP = 2
ASM_BLOCKS = 8
GROUPS = 8
SIDE = 4
WIDTH = 384
BLOCK = 256
HALF = BLOCK // 2
CHUNK = BLOCK // 4
LAG = 6
NEAR = 3 * LAG
FAR = 5 * LAG
TAIL = 7
BLOCKS = 24
F32 = jnp.float32
BF16 = jnp.bfloat16

STEPS = ((1, 0), (0, 1), (-1, 0), (0, -1))
PARENT = {
    (1, 0): 0, (2, 0): 0, (3, 0): 0, (0, 1): 2, (1, 1): 1, (2, 1): 0, (3, 1): 0, (0, 2): 2,
    (1, 2): 1, (2, 2): 1, (3, 2): 0, (0, 3): 2, (1, 3): 3, (2, 3): 3, (3, 3): 0,
}
SENDERS = tuple(
    sorted(
        ((x - STEPS[way][0]) % SIDE) + SIDE * ((z - STEPS[way][1]) % SIDE)
        for (x, z), own in PARENT.items()
        if own == way
    )
    for way in range(4)
)


def depth_of(node):
    depth = 0
    while node != (0, 0):
        step = STEPS[PARENT[node]]
        node = ((node[0] - step[0]) % SIDE, (node[1] - step[1]) % SIDE)
        depth += 1
    return depth


DEPTH = {x + SIDE * z: depth_of((x, z)) for x, z in PARENT}


def pieces(block):
    if block < TICKS:
        return ((block * WIDTH, BLOCK),)
    if block < 8:
        return ((5376 + (block - TICKS) * BLOCK, BLOCK),)
    if block < 10:
        first = (block - 8) * 2 * WIDTH + P_SIZE
        return ((first, HALF), (first + WIDTH, HALF))
    return ((1792 + (block - 10) * BLOCK, BLOCK),)


def number(tick):
    return BLOCKS - 1 - tick


FIRST_SLOT = tuple(sum(number(tick) for tick in range(last)) for last in range(TICKS))


def split(value):
    high = value.astype(BF16)
    return high, (value - high.astype(F32)).astype(BF16)


def dot(a, b):
    return jnp.dot(a, b, preferred_element_type=F32)


def dot3(a, b):
    return dot(a[0], b[0]) + dot(a[0], b[1]) + dot(a[1], b[0])


def kernel(
    front, dest, target, rows, arrived, tags, panel, urows, inv_high, inv_low, cont, picked, labels,
    load_sem, send_sem, recv_sem, slot_send, slot_recv, tag_send, tag_recv,
):
    me = lax.axis_index("blk")
    mine = lax.axis_index("front")
    x = lax.rem(me, SIDE)
    z = lax.div(me, SIDE)
    around = [
        z * SIDE + lax.rem(x + 1, SIDE),
        lax.rem(z + 1, SIDE) * SIDE + x,
        z * SIDE + lax.rem(x + SIDE - 1, SIDE),
        lax.rem(z + SIDE - 1, SIDE) * SIDE + x,
    ]

    for block in range(BLOCKS):
        at = 0
        for start, size in pieces(block):
            pltpu.make_async_copy(
                front.at[pl.ds(start, size)], rows.at[block, pl.ds(at, size)], load_sem.at[block]
            ).start()
            at += size

    barrier = pltpu.get_barrier_semaphore()
    for other in around:
        pl.semaphore_signal(barrier, inc=1, device_id={"blk": other}, device_id_type=pl.DeviceIdType.MESH)
    for offset in range(1, GROUPS):
        pl.semaphore_signal(
            barrier,
            inc=1,
            device_id={"front": lax.rem(mine + offset, GROUPS)},
            device_id_type=pl.DeviceIdType.MESH,
        )
    pl.semaphore_wait(barrier, 4 + GROUPS - 1)

    def place(tick):
        dx = lax.rem(x - tick % SIDE + SIDE, SIDE)
        dz = lax.rem(z - tick // SIDE + SIDE, SIDE)
        nx, nz = lax.rem(SIDE - dx, SIDE), lax.rem(SIDE - dz, SIDE)
        turned = (dx + SIDE * dz, dz + SIDE * nx, nx + SIDE * nz, nz + SIDE * dx)
        result = []
        lags = []
        for tree in range(4):
            ways = []
            for way in range(4):
                has = turned[tree] == SENDERS[(way - tree) % 4][0]
                for node in SENDERS[(way - tree) % 4][1:]:
                    has = has | (turned[tree] == node)
                ways.append(has)
            result.append(ways)
            lag = jnp.int32(0)
            for node, depth in DEPTH.items():
                lag = jnp.where(turned[tree] == node, depth * LAG, lag)
            lags.append(lag)
        deepest = jnp.maximum(jnp.maximum(lags[0], lags[1]), jnp.maximum(lags[2], lags[3]))
        deepest = jnp.maximum(deepest, NEAR)
        return result, lags, deepest

    places = [place(tick) for tick in range(TICKS)]

    def chunk_copy(tick, block, tree, way):
        chunk = panel.at[tick, block, pl.ds(tree * CHUNK, CHUNK)]
        return pltpu.make_async_remote_copy(
            src_ref=chunk,
            dst_ref=chunk,
            send_sem=send_sem.at[tick, way],
            recv_sem=recv_sem.at[tick, block, tree],
            device_id={"blk": around[way]},
            device_id_type=pl.DeviceIdType.MESH,
        )

    def send(tick, block, tree):
        for way in range(4):
            @pl.when(places[tick][0][tree][way])
            def _():
                chunk_copy(tick, block, tree, way).start()

    def forward(tick, slot):
        for tree in range(4):
            index = slot - places[tick][1][tree]

            @pl.when((me != tick) & (index >= 0) & (index < number(tick)))
            def _():
                block = tick + 1 + index
                chunk_copy(tick, block, tree, 0).wait_recv()
                send(tick, block, tree)

    def wait_load(block):
        pltpu.make_async_copy(front.at[pl.ds(0, BLOCK)], rows.at[block], load_sem.at[block]).wait()

    def invert(tick):
        matrix = rows[tick, :, :P_SIZE]
        line = lax.broadcasted_iota(jnp.int32, (P_SIZE, P_SIZE), 0)
        column = lax.broadcasted_iota(jnp.int32, (P_SIZE, P_SIZE), 1)
        eye = line == column
        on_diagonal = jnp.where(eye, matrix, 0.0)
        by_row = 1.0 / jnp.sum(on_diagonal, axis=1, keepdims=True)
        by_column = 1.0 / jnp.sum(on_diagonal, axis=0, keepdims=True)
        first = jnp.where(eye, 2.0 * by_row, 0.0) - by_row * matrix * by_column
        first = split(first)
        residual = jnp.where(eye, 2.0, 0.0) - dot3(split(matrix), first)
        high, low = split(dot3(first, split(residual)))
        inv_high[...] = high
        inv_low[...] = low

    def multiply(tick, block):
        mult = dot3(split(rows[block, :, :P_SIZE]), (inv_high[...], inv_low[...]))
        rows[block, :, :P_SIZE] = mult
        panel[tick, block] = mult.astype(BF16)

    def pivot_rows(tick):
        keep = jnp.where(me > tick, 1.0, 0.0).astype(F32)
        urows[tick, :, :P_SIZE] = (rows[tick, :, :P_SIZE] * keep).astype(BF16)
        urows[tick, :, P_SIZE:] = rows[tick, :, P_SIZE:].astype(BF16)

    def loop(first, last, body):
        def step(index, carry):
            body(index)
            return carry

        lax.fori_loop(first, last, step, 0)

    wait_load(0)

    @pl.when(me == 0)
    def _():
        invert(0)

        def own(block):
            wait_load(block)
            multiply(0, block)
            for tree in range(4):
                send(0, block, tree)

        loop(1, BLOCKS, own)

    def slot_copy(offset):
        peer = lax.rem(mine + offset, GROUPS)
        return pltpu.make_async_remote_copy(
            src_ref=picked.at[peer],
            dst_ref=arrived.at[mine],
            send_sem=slot_send.at[offset],
            recv_sem=slot_recv.at[offset],
            device_id={"front": peer},
            device_id_type=pl.DeviceIdType.MESH,
        )

    def tag_copy(offset):
        peer = lax.rem(mine + offset, GROUPS)
        return pltpu.make_async_remote_copy(
            src_ref=labels.at[peer],
            dst_ref=tags.at[mine],
            send_sem=tag_send.at[offset],
            recv_sem=tag_recv.at[offset],
            device_id={"front": peer},
            device_id_type=pl.DeviceIdType.MESH,
        )

    slots = []
    for block in range(NB):
        slot = jnp.int32(0)
        for before in range(block):
            slot = slot + jnp.where(dest[before] == dest[block], 1, 0)
        slots.append(slot)
    lane = lax.broadcasted_iota(jnp.int32, (1, 128), 1)
    for group in range(GROUPS):
        label = jnp.full((1, 128), -1, jnp.int32)
        for block in range(NB):
            label = jnp.where(lane == jnp.where(dest[block] == group, slots[block], -1), target[block], label)
        labels[group] = label
    tags[mine] = labels[mine]
    for offset in range(1, GROUPS):
        tag_copy(offset).start()

    def exchange():
        keep = jnp.where(me >= TICKS, 1.0, 0.0).astype(F32)
        for block in range(NB):
            part = pl.ds(block % 2 * RB, RB)
            cont[block, :, :P_SIZE] = (rows[TICKS + block // 2, part, :P_SIZE] * keep).astype(BF16)
            cont[block, :, P_SIZE:] = rows[TICKS + block // 2, part, P_SIZE:].astype(BF16)
        cont[NB] = jnp.zeros((RB, WIDTH), BF16)
        for group in range(GROUPS):
            for slot in range(CAP):
                number_of = jnp.int32(NB)
                for block in range(NB):
                    number_of = jnp.where((dest[block] == group) & (slots[block] == slot), block, number_of)
                picked[group, slot] = cont[number_of]
        for offset in (4, 3, 5, 2, 6, 1, 7):
            slot_copy(offset).start()
        arrived[mine] = picked[mine]

    def update(tick, index, first):
        @pl.when((index >= 0) & (index < number(tick)))
        def _():
            block = tick + 1 + index
            if first:
                @pl.when(index == 0)
                def _():
                    pivot_rows(tick)

            if tick == 0:
                @pl.when(me != 0)
                def _():
                    wait_load(block)

            rows[block] = rows[block] - dot(panel[tick, block], urows[tick])
            if tick + 1 < TICKS:
                @pl.when(me == tick + 1)
                def _():
                    if first:
                        @pl.when(index == 0)
                        def _():
                            invert(tick + 1)

                    @pl.when(index > 0)
                    def _():
                        multiply(tick + 1, block)
                        for tree in range(4):
                            send(tick + 1, block, tree)
            elif first:
                @pl.when(block == TAIL)
                def _():
                    exchange()

    ends = [FIRST_SLOT[tick] + number(tick) + FAR for tick in range(TICKS)]
    starts = [FIRST_SLOT[tick] + NEAR for tick in range(TICKS)]
    firsts = [FIRST_SLOT[tick] + FAR + 3 for tick in range(TICKS)]
    marks = sorted(set(list(FIRST_SLOT) + ends + starts + firsts))
    for begin, end in zip(marks[:-1], marks[1:]):
        def step(slot):
            for tick in range(TICKS):
                if FIRST_SLOT[tick] <= begin < ends[tick]:
                    forward(tick, slot - FIRST_SLOT[tick])
            for tick in range(TICKS):
                if starts[tick] <= begin < ends[tick]:
                    update(tick, slot - FIRST_SLOT[tick] - places[tick][2], begin < firsts[tick])

        loop(begin, end, step)

    for offset in range(1, GROUPS):
        slot_copy(offset).wait()
        tag_copy(offset).wait()
    for tick in range(TICKS):
        for way in range(4):
            used = places[tick][0][0][way]
            for tree in range(1, 4):
                used = used | places[tick][0][tree][way]

            @pl.when(used)
            def _():
                sent = panel.at[tick, pl.ds(0, number(tick)), pl.ds(0, CHUNK)]
                pltpu.make_async_remote_copy(
                    src_ref=sent,
                    dst_ref=sent,
                    send_sem=send_sem.at[tick, way],
                    recv_sem=recv_sem.at[tick, 0, 0],
                    device_id={"blk": around[way]},
                    device_id_type=pl.DeviceIdType.MESH,
                ).wait_send()


def factor(front, dest, target):
    return pl.pallas_call(
        kernel,
        out_shape=(
            pltpu.VMEM((BLOCKS, BLOCK, WIDTH), F32),
            pltpu.VMEM((GROUPS, CAP, RB, WIDTH), BF16),
            jax.ShapeDtypeStruct((GROUPS, 1, 128), jnp.int32),
        ),
        in_specs=[
            pl.BlockSpec(memory_space=pl.ANY),
            pl.BlockSpec(memory_space=pltpu.SMEM),
            pl.BlockSpec(memory_space=pltpu.SMEM),
        ],
        out_specs=(
            pl.BlockSpec(memory_space=pltpu.VMEM),
            pl.BlockSpec(memory_space=pltpu.VMEM),
            pl.BlockSpec(memory_space=pltpu.VMEM),
        ),
        scratch_shapes=[
            pltpu.VMEM((TICKS, BLOCKS, BLOCK, P_SIZE), BF16),
            pltpu.VMEM((TICKS, P_SIZE, WIDTH), BF16),
            pltpu.VMEM((P_SIZE, P_SIZE), BF16),
            pltpu.VMEM((P_SIZE, P_SIZE), BF16),
            pltpu.VMEM((NB + 1, RB, WIDTH), BF16),
            pltpu.VMEM((GROUPS, CAP, RB, WIDTH), BF16),
            pltpu.VMEM((GROUPS, 1, 128), jnp.int32),
            pltpu.SemaphoreType.DMA((BLOCKS,)),
            pltpu.SemaphoreType.DMA((TICKS, 4)),
            pltpu.SemaphoreType.DMA((TICKS, BLOCKS, 4)),
            pltpu.SemaphoreType.DMA((GROUPS,)),
            pltpu.SemaphoreType.DMA((GROUPS,)),
            pltpu.SemaphoreType.DMA((GROUPS,)),
            pltpu.SemaphoreType.DMA((GROUPS,)),
        ],
        compiler_params=pltpu.CompilerParams(
            collective_id=0, has_side_effects=True, vmem_limit_bytes=45 * 1024 * 1024
        ),
        name="factor",
    )(front, dest, target)


def finish_kernel(rows, arrived, tags, base, factored, assembled, total, rows_sem, base_sem, out_sem):
    load = pltpu.make_async_copy(base, total, base_sem)
    load.start()
    copies = []
    for block in range(BLOCKS):
        at = 0
        for start, size in pieces(block):
            copies.append(
                pltpu.make_async_copy(
                    rows.at[block, pl.ds(at, size)], factored.at[pl.ds(start, size)], rows_sem.at[len(copies)]
                )
            )
            copies[-1].start()
            at += size
    load.wait()
    for group in range(GROUPS):
        for slot in range(CAP):
            place = tags[group, 0, slot]

            @pl.when(place >= 0)
            def _():
                part = pl.ds(pl.multiple_of(place * RB, RB), RB)
                total[part] = total[part] + arrived[group, slot].astype(F32)

    store = pltpu.make_async_copy(total, assembled, out_sem)
    store.start()
    for copy in copies:
        copy.wait()
    store.wait()


def finish(rows, arrived, tags, base, shape):
    return pl.pallas_call(
        finish_kernel,
        out_shape=(jax.ShapeDtypeStruct(shape, F32), jax.ShapeDtypeStruct(base.shape, F32)),
        in_specs=[
            pl.BlockSpec(memory_space=pltpu.VMEM),
            pl.BlockSpec(memory_space=pltpu.VMEM),
            pl.BlockSpec(memory_space=pltpu.SMEM),
            pl.BlockSpec(memory_space=pl.ANY),
        ],
        out_specs=(pl.BlockSpec(memory_space=pl.ANY), pl.BlockSpec(memory_space=pl.ANY)),
        scratch_shapes=[
            pltpu.VMEM((ASM_BLOCKS * RB, WIDTH), F32),
            pltpu.SemaphoreType.DMA((BLOCKS + 2,)),
            pltpu.SemaphoreType.DMA,
            pltpu.SemaphoreType.DMA,
        ],
        compiler_params=pltpu.CompilerParams(vmem_limit_bytes=16 * 1024 * 1024),
        name="finish",
    )(rows, arrived, tags, base)


def local(front, parent_group, row_block, parent_base):
    rows, arrived, tags = factor(front, parent_group.reshape(NB), row_block.reshape(NB))
    return finish(rows, arrived, tags, parent_base, front.shape)


def solution(mesh):
    placed = (
        P("front", "blk"),
        P("front", "blk", None, None),
        P("front", "blk", None),
        P("front", "blk"),
    )
    return jax.shard_map(
        local,
        mesh=mesh,
        in_specs=placed,
        out_specs=(P("front", "blk"), P("front", "blk")),
        check_vma=False,
    )
```

```python
import jax
import jax.numpy as jnp
from jax import lax
from jax.experimental import pallas as pl
from jax.experimental.pallas import tpu as pltpu
from jax.sharding import PartitionSpec as P

P_SIZE = 256
TICKS = 5
RB = 128
NB = 6
CAP = 2
ASM_BLOCKS = 8
GROUPS = 8
SIDE = 4
WIDTH = 384
BLOCK = 256
HALF = BLOCK // 2
CHUNK = BLOCK // 4
LAGS = (0, 4, 10, 16, 22, 28)
FIRST_SLOT = (0, 17, 34, 53, 78)
LEAST = 13
UPDATES = tuple(max(LEAST, LAGS[depth]) for depth in (0, 3, 4, 5))
TAIL = 7
BLOCKS = 24
F32 = jnp.float32
BF16 = jnp.bfloat16

STEPS = ((1, 0), (0, 1), (-1, 0), (0, -1))
PARENT = {
    (1, 0): 0, (2, 0): 0, (3, 0): 0, (0, 1): 2, (1, 1): 1, (2, 1): 0, (3, 1): 0, (0, 2): 2,
    (1, 2): 1, (2, 2): 1, (3, 2): 0, (0, 3): 2, (1, 3): 3, (2, 3): 3, (3, 3): 0,
}
SENDERS = tuple(
    sorted(
        ((x - STEPS[way][0]) % SIDE) + SIDE * ((z - STEPS[way][1]) % SIDE)
        for (x, z), own in PARENT.items()
        if own == way
    )
    for way in range(4)
)


def depth_of(node):
    depth = 0
    while node != (0, 0):
        step = STEPS[PARENT[node]]
        node = ((node[0] - step[0]) % SIDE, (node[1] - step[1]) % SIDE)
        depth += 1
    return depth


DEPTH = {x + SIDE * z: depth_of((x, z)) for x, z in PARENT}


def pieces(block):
    if block < TICKS:
        return ((block * WIDTH, BLOCK),)
    if block < 8:
        return ((5376 + (block - TICKS) * BLOCK, BLOCK),)
    if block < 10:
        first = (block - 8) * 2 * WIDTH + P_SIZE
        return ((first, HALF), (first + WIDTH, HALF))
    return ((1792 + (block - 10) * BLOCK, BLOCK),)


def number(tick):
    return BLOCKS - 1 - tick


def split(value):
    high = value.astype(BF16)
    return high, (value - high.astype(F32)).astype(BF16)


def dot(a, b):
    return jnp.dot(a, b, preferred_element_type=F32)


def dot3(a, b):
    return dot(a[0], b[0]) + dot(a[0], b[1]) + dot(a[1], b[0])


def kernel(
    front, dest, target, rows, arrived, tags, panel, urows, inv_high, inv_low, cont, picked, labels,
    load_sem, send_sem, recv_sem, slot_send, slot_recv, tag_send, tag_recv,
):
    me = lax.axis_index("blk")
    mine = lax.axis_index("front")
    x = lax.rem(me, SIDE)
    z = lax.div(me, SIDE)
    around = [
        z * SIDE + lax.rem(x + 1, SIDE),
        lax.rem(z + 1, SIDE) * SIDE + x,
        z * SIDE + lax.rem(x + SIDE - 1, SIDE),
        lax.rem(z + SIDE - 1, SIDE) * SIDE + x,
    ]

    barrier = pltpu.get_barrier_semaphore()
    for other in around:
        pl.semaphore_signal(barrier, inc=1, device_id={"blk": other}, device_id_type=pl.DeviceIdType.MESH)
    for offset in range(1, GROUPS):
        pl.semaphore_signal(
            barrier,
            inc=1,
            device_id={"front": lax.rem(mine + offset, GROUPS)},
            device_id_type=pl.DeviceIdType.MESH,
        )

    def load(block):
        at = 0
        for start, size in pieces(block):
            pltpu.make_async_copy(
                front.at[pl.ds(start, size)], rows.at[block, pl.ds(at, size)], load_sem.at[block]
            ).start()
            at += size

    load(0)

    def place(tick):
        dx = lax.rem(x - tick % SIDE + SIDE, SIDE)
        dz = lax.rem(z - tick // SIDE + SIDE, SIDE)
        nx, nz = lax.rem(SIDE - dx, SIDE), lax.rem(SIDE - dz, SIDE)
        turned = (dx + SIDE * dz, dz + SIDE * nx, nx + SIDE * nz, nz + SIDE * dx)
        result = []
        lags = []
        for tree in range(4):
            ways = []
            for way in range(4):
                has = turned[tree] == SENDERS[(way - tree) % 4][0]
                for node in SENDERS[(way - tree) % 4][1:]:
                    has = has | (turned[tree] == node)
                ways.append(has)
            result.append(ways)
            lag = jnp.int32(0)
            for node, depth in DEPTH.items():
                lag = jnp.where(turned[tree] == node, LAGS[depth], lag)
            lags.append(lag)
        deepest = jnp.maximum(jnp.maximum(lags[0], lags[1]), jnp.maximum(lags[2], lags[3]))
        deepest = jnp.maximum(deepest, LEAST)
        return result, lags, deepest

    places = [place(tick) for tick in range(TICKS)]

    def chunk_copy(tick, block, tree, way):
        chunk = panel.at[tick, block, pl.ds(tree * CHUNK, CHUNK)]
        return pltpu.make_async_remote_copy(
            src_ref=chunk,
            dst_ref=chunk,
            send_sem=send_sem.at[tick, way],
            recv_sem=recv_sem.at[tick, block, tree],
            device_id={"blk": around[way]},
            device_id_type=pl.DeviceIdType.MESH,
        )

    def send(tick, block, tree):
        for way in range(4):
            @pl.when(places[tick][0][tree][way])
            def _():
                chunk_copy(tick, block, tree, way).start()

    def forward(tick, slot):
        for tree in range(4):
            index = slot - places[tick][1][tree]

            @pl.when((me != tick) & (index >= 0) & (index < number(tick)))
            def _():
                block = tick + 1 + index
                chunk_copy(tick, block, tree, 0).wait_recv()
                send(tick, block, tree)

    def wait_load(block):
        pltpu.make_async_copy(front.at[pl.ds(0, BLOCK)], rows.at[block], load_sem.at[block]).wait()

    def invert(tick):
        matrix = rows[tick, :, :P_SIZE]
        line = lax.broadcasted_iota(jnp.int32, (P_SIZE, P_SIZE), 0)
        column = lax.broadcasted_iota(jnp.int32, (P_SIZE, P_SIZE), 1)
        eye = line == column
        on_diagonal = jnp.where(eye, matrix, 0.0)
        by_row = 1.0 / jnp.sum(on_diagonal, axis=1, keepdims=True)
        by_column = 1.0 / jnp.sum(on_diagonal, axis=0, keepdims=True)
        first = jnp.where(eye, 2.0 * by_row, 0.0) - by_row * matrix * by_column
        first = split(first)
        residual = jnp.where(eye, 2.0, 0.0) - dot3(split(matrix), first)
        high, low = split(dot3(first, split(residual)))
        inv_high[...] = high
        inv_low[...] = low

    def multiply(tick, block):
        mult = dot3(split(rows[block, :, :P_SIZE]), (inv_high[...], inv_low[...]))
        rows[block, :, :P_SIZE] = mult
        panel[tick, block] = mult.astype(BF16)

    def pivot_rows(tick):
        keep = jnp.where(me > tick, 1.0, 0.0).astype(F32)
        urows[tick, :, :P_SIZE] = (rows[tick, :, :P_SIZE] * keep).astype(BF16)
        urows[tick, :, P_SIZE:] = rows[tick, :, P_SIZE:].astype(BF16)

    def loop(first, last, body):
        def step(index, carry):
            body(index)
            return carry

        lax.fori_loop(first, last, step, 0)

    wait_load(0)
    for block in range(1, BLOCKS):
        load(block)

    @pl.when(me == 0)
    def _():
        invert(0)

    pl.semaphore_wait(barrier, 4 + GROUPS - 1)

    @pl.when(me == 0)
    def _():
        def own(block):
            wait_load(block)
            multiply(0, block)
            for tree in range(4):
                send(0, block, tree)

        loop(1, BLOCKS, own)

    def slot_copy(offset):
        peer = lax.rem(mine + offset, GROUPS)
        return pltpu.make_async_remote_copy(
            src_ref=picked.at[peer],
            dst_ref=arrived.at[mine],
            send_sem=slot_send.at[offset],
            recv_sem=slot_recv.at[offset],
            device_id={"front": peer},
            device_id_type=pl.DeviceIdType.MESH,
        )

    def tag_copy(offset):
        peer = lax.rem(mine + offset, GROUPS)
        return pltpu.make_async_remote_copy(
            src_ref=labels.at[peer],
            dst_ref=tags.at[mine],
            send_sem=tag_send.at[offset],
            recv_sem=tag_recv.at[offset],
            device_id={"front": peer},
            device_id_type=pl.DeviceIdType.MESH,
        )

    slots = []
    for block in range(NB):
        slot = jnp.int32(0)
        for before in range(block):
            slot = slot + jnp.where(dest[before] == dest[block], 1, 0)
        slots.append(slot)
    lane = lax.broadcasted_iota(jnp.int32, (1, 128), 1)
    for group in range(GROUPS):
        label = jnp.full((1, 128), -1, jnp.int32)
        for block in range(NB):
            label = jnp.where(lane == jnp.where(dest[block] == group, slots[block], -1), target[block], label)
        labels[group] = label
    tags[mine] = labels[mine]
    for offset in range(1, GROUPS):
        tag_copy(offset).start()

    def exchange():
        keep = jnp.where(me >= TICKS, 1.0, 0.0).astype(F32)
        for block in range(NB):
            part = pl.ds(block % 2 * RB, RB)
            cont[block, :, :P_SIZE] = (rows[TICKS + block // 2, part, :P_SIZE] * keep).astype(BF16)
            cont[block, :, P_SIZE:] = rows[TICKS + block // 2, part, P_SIZE:].astype(BF16)
        cont[NB] = jnp.zeros((RB, WIDTH), BF16)
        for group in range(GROUPS):
            for slot in range(CAP):
                number_of = jnp.int32(NB)
                for block in range(NB):
                    number_of = jnp.where((dest[block] == group) & (slots[block] == slot), block, number_of)
                picked[group, slot] = cont[number_of]
        for offset in (4, 3, 5, 2, 6, 1, 7):
            slot_copy(offset).start()
        arrived[mine] = picked[mine]

    def update(tick, index, first):
        @pl.when((index >= 0) & (index < number(tick)))
        def _():
            block = tick + 1 + index
            if first:
                @pl.when(index == 0)
                def _():
                    pivot_rows(tick)

            if tick == 0:
                @pl.when(me != 0)
                def _():
                    wait_load(block)

            rows[block] = rows[block] - dot(panel[tick, block], urows[tick])
            if tick + 1 < TICKS:
                @pl.when(me == tick + 1)
                def _():
                    if first:
                        @pl.when(index == 0)
                        def _():
                            invert(tick + 1)

                    @pl.when(index > 0)
                    def _():
                        multiply(tick + 1, block)
                        for tree in range(4):
                            send(tick + 1, block, tree)
            elif first:
                @pl.when(block == TAIL)
                def _():
                    exchange()

    moves = [(FIRST_SLOT[tick] + LAGS[1], FIRST_SLOT[tick] + number(tick) + LAGS[5]) for tick in range(TICKS)]
    works = [(FIRST_SLOT[tick] + min(UPDATES), FIRST_SLOT[tick] + number(tick) + max(UPDATES)) for tick in range(TICKS)]
    firsts = [FIRST_SLOT[tick] + max(UPDATES) + 3 for tick in range(TICKS)]
    marks = sorted({mark for pair in moves + works for mark in pair} | set(firsts))
    for begin, end in zip(marks[:-1], marks[1:]):
        def step(slot):
            for tick in range(TICKS):
                if moves[tick][0] <= begin < moves[tick][1]:
                    forward(tick, slot - FIRST_SLOT[tick])
            for tick in range(TICKS):
                if works[tick][0] <= begin < works[tick][1]:
                    update(tick, slot - FIRST_SLOT[tick] - places[tick][2], begin < firsts[tick])

        loop(begin, end, step)

    for offset in range(1, GROUPS):
        slot_copy(offset).wait()
        tag_copy(offset).wait()
    for tick in range(TICKS):
        for way in range(4):
            used = places[tick][0][0][way]
            for tree in range(1, 4):
                used = used | places[tick][0][tree][way]

            @pl.when(used)
            def _():
                sent = panel.at[tick, pl.ds(0, number(tick)), pl.ds(0, CHUNK)]
                pltpu.make_async_remote_copy(
                    src_ref=sent,
                    dst_ref=sent,
                    send_sem=send_sem.at[tick, way],
                    recv_sem=recv_sem.at[tick, 0, 0],
                    device_id={"blk": around[way]},
                    device_id_type=pl.DeviceIdType.MESH,
                ).wait_send()


def factor(front, dest, target):
    return pl.pallas_call(
        kernel,
        out_shape=(
            pltpu.VMEM((BLOCKS, BLOCK, WIDTH), F32),
            pltpu.VMEM((GROUPS, CAP, RB, WIDTH), BF16),
            pltpu.VMEM((GROUPS, 1, 128), jnp.int32),
        ),
        in_specs=[
            pl.BlockSpec(memory_space=pl.ANY),
            pl.BlockSpec(memory_space=pltpu.SMEM),
            pl.BlockSpec(memory_space=pltpu.SMEM),
        ],
        out_specs=(
            pl.BlockSpec(memory_space=pltpu.VMEM),
            pl.BlockSpec(memory_space=pltpu.VMEM),
            pl.BlockSpec(memory_space=pltpu.VMEM),
        ),
        scratch_shapes=[
            pltpu.VMEM((TICKS, BLOCKS, BLOCK, P_SIZE), BF16),
            pltpu.VMEM((TICKS, P_SIZE, WIDTH), BF16),
            pltpu.VMEM((P_SIZE, P_SIZE), BF16),
            pltpu.VMEM((P_SIZE, P_SIZE), BF16),
            pltpu.VMEM((NB + 1, RB, WIDTH), BF16),
            pltpu.VMEM((GROUPS, CAP, RB, WIDTH), BF16),
            pltpu.VMEM((GROUPS, 1, 128), jnp.int32),
            pltpu.SemaphoreType.DMA((BLOCKS,)),
            pltpu.SemaphoreType.DMA((TICKS, 4)),
            pltpu.SemaphoreType.DMA((TICKS, BLOCKS, 4)),
            pltpu.SemaphoreType.DMA((GROUPS,)),
            pltpu.SemaphoreType.DMA((GROUPS,)),
            pltpu.SemaphoreType.DMA((GROUPS,)),
            pltpu.SemaphoreType.DMA((GROUPS,)),
        ],
        compiler_params=pltpu.CompilerParams(
            collective_id=0, has_side_effects=True, vmem_limit_bytes=45 * 1024 * 1024
        ),
        name="factor",
    )(front, dest, target)


def finish_kernel(
    rows, arrived, tags, base, factored, assembled, labels, tags_sem, total, rows_sem, base_sem, out_sem
):
    read = pltpu.make_async_copy(tags, labels, tags_sem)
    read.start()
    load = pltpu.make_async_copy(base, total, base_sem)
    load.start()
    copies = []
    for block in range(BLOCKS):
        at = 0
        for start, size in pieces(block):
            copies.append(
                pltpu.make_async_copy(
                    rows.at[block, pl.ds(at, size)], factored.at[pl.ds(start, size)], rows_sem.at[len(copies)]
                )
            )
            copies[-1].start()
            at += size
    load.wait()
    read.wait()
    for group in range(GROUPS):
        for slot in range(CAP):
            place = labels[group, 0, slot]

            @pl.when(place >= 0)
            def _():
                part = pl.ds(pl.multiple_of(place * RB, RB), RB)
                total[part] = total[part] + arrived[group, slot].astype(F32)

    store = pltpu.make_async_copy(total, assembled, out_sem)
    store.start()
    for copy in copies:
        copy.wait()
    store.wait()


def finish(rows, arrived, tags, base, shape):
    return pl.pallas_call(
        finish_kernel,
        out_shape=(jax.ShapeDtypeStruct(shape, F32), jax.ShapeDtypeStruct(base.shape, F32)),
        in_specs=[
            pl.BlockSpec(memory_space=pltpu.VMEM),
            pl.BlockSpec(memory_space=pltpu.VMEM),
            pl.BlockSpec(memory_space=pltpu.VMEM),
            pl.BlockSpec(memory_space=pl.ANY),
        ],
        out_specs=(pl.BlockSpec(memory_space=pl.ANY), pl.BlockSpec(memory_space=pl.ANY)),
        scratch_shapes=[
            pltpu.SMEM((GROUPS, 1, 128), jnp.int32),
            pltpu.SemaphoreType.DMA,
            pltpu.VMEM((ASM_BLOCKS * RB, WIDTH), F32),
            pltpu.SemaphoreType.DMA((BLOCKS + 2,)),
            pltpu.SemaphoreType.DMA,
            pltpu.SemaphoreType.DMA,
        ],
        compiler_params=pltpu.CompilerParams(vmem_limit_bytes=16 * 1024 * 1024),
        name="finish",
    )(rows, arrived, tags, base)


def local(front, parent_group, row_block, parent_base):
    rows, arrived, tags = factor(front, parent_group.reshape(NB), row_block.reshape(NB))
    return finish(rows, arrived, tags, parent_base, front.shape)


def solution(mesh):
    placed = (
        P("front", "blk"),
        P("front", "blk", None, None),
        P("front", "blk", None),
        P("front", "blk"),
    )
    return jax.shard_map(
        local,
        mesh=mesh,
        in_specs=placed,
        out_specs=(P("front", "blk"), P("front", "blk")),
        check_vma=False,
    )
```

```python
import jax
import jax.numpy as jnp
from jax import lax
from jax.experimental import pallas as pl
from jax.experimental.pallas import tpu as pltpu
from jax.sharding import PartitionSpec as P

P_SIZE = 256
TICKS = 5
RB = 128
NB = 6
CAP = 2
ASM_BLOCKS = 8
GROUPS = 8
SIDE = 4
WIDTH = 384
BLOCK = 256
HALF = BLOCK // 2
CHUNK = BLOCK // 4
LAGS = (
    (0, 2, 8, 13, 22, 28),
    (0, 5, 6, 15, 20, 26),
    (0, 2, 9, 16, 21, 34),
    (0, 1, 8, 12, 15, 30),
    (0, 1, 4, 12, 13, 19),
)
FIRST_SLOT = (0, 28, 43, 66, 85)
LEAST = (22, 3, 10, 15, 3)
IDLE = 1000
UPDATES = tuple(tuple(max(LEAST[tick], LAGS[tick][depth]) for depth in (0, 3, 4, 5)) for tick in range(TICKS))
TAIL = 7
BLOCKS = 24
F32 = jnp.float32
BF16 = jnp.bfloat16

STEPS = ((1, 0), (0, 1), (-1, 0), (0, -1))
PARENT = {
    (1, 0): 0, (2, 0): 0, (3, 0): 0, (0, 1): 2, (1, 1): 1, (2, 1): 0, (3, 1): 0, (0, 2): 2,
    (1, 2): 1, (2, 2): 1, (3, 2): 0, (0, 3): 2, (1, 3): 3, (2, 3): 3, (3, 3): 0,
}
SENDERS = tuple(
    sorted(
        ((x - STEPS[way][0]) % SIDE) + SIDE * ((z - STEPS[way][1]) % SIDE)
        for (x, z), own in PARENT.items()
        if own == way
    )
    for way in range(4)
)


def depth_of(node):
    depth = 0
    while node != (0, 0):
        step = STEPS[PARENT[node]]
        node = ((node[0] - step[0]) % SIDE, (node[1] - step[1]) % SIDE)
        depth += 1
    return depth


DEPTH = {x + SIDE * z: depth_of((x, z)) for x, z in PARENT}


def pieces(block):
    if block < TICKS:
        return ((block * WIDTH, BLOCK),)
    if block < 8:
        return ((5376 + (block - TICKS) * BLOCK, BLOCK),)
    if block < 10:
        first = (block - 8) * 2 * WIDTH + P_SIZE
        return ((first, HALF), (first + WIDTH, HALF))
    return ((1792 + (block - 10) * BLOCK, BLOCK),)


def number(tick):
    return BLOCKS - 1 - tick


def split(value):
    high = value.astype(BF16)
    return high, (value - high.astype(F32)).astype(BF16)


def dot(a, b):
    return jnp.dot(a, b, preferred_element_type=F32)


def left(value):
    high, low = split(value)
    return jnp.concatenate([high, high, low], axis=1)


def right(value):
    high, low = split(value)
    return jnp.concatenate([high, low, high], axis=0)


def kernel(
    front, dest, target, rows, arrived, tags, panel, urows, inverse, cont, picked, labels,
    load_sem, send_sem, recv_sem, slot_send, slot_recv, tag_send, tag_recv,
):
    me = lax.axis_index("blk")
    mine = lax.axis_index("front")
    x = lax.rem(me, SIDE)
    z = lax.div(me, SIDE)
    around = [
        z * SIDE + lax.rem(x + 1, SIDE),
        lax.rem(z + 1, SIDE) * SIDE + x,
        z * SIDE + lax.rem(x + SIDE - 1, SIDE),
        lax.rem(z + SIDE - 1, SIDE) * SIDE + x,
    ]

    barrier = pltpu.get_barrier_semaphore()
    for other in around:
        pl.semaphore_signal(barrier, inc=1, device_id={"blk": other}, device_id_type=pl.DeviceIdType.MESH)
    for offset in range(1, GROUPS):
        pl.semaphore_signal(
            barrier,
            inc=1,
            device_id={"front": lax.rem(mine + offset, GROUPS)},
            device_id_type=pl.DeviceIdType.MESH,
        )

    def load(block):
        at = 0
        for start, size in pieces(block):
            pltpu.make_async_copy(
                front.at[pl.ds(start, size)], rows.at[block, pl.ds(at, size)], load_sem.at[block]
            ).start()
            at += size

    load(0)

    def place(tick):
        dx = lax.rem(x - tick % SIDE + SIDE, SIDE)
        dz = lax.rem(z - tick // SIDE + SIDE, SIDE)
        nx, nz = lax.rem(SIDE - dx, SIDE), lax.rem(SIDE - dz, SIDE)
        turned = (dx + SIDE * dz, dz + SIDE * nx, nx + SIDE * nz, nz + SIDE * dx)
        result = []
        lags = []
        for tree in range(4):
            ways = []
            for way in range(4):
                has = turned[tree] == SENDERS[(way - tree) % 4][0]
                for node in SENDERS[(way - tree) % 4][1:]:
                    has = has | (turned[tree] == node)
                ways.append(has)
            result.append(ways)
            lag = jnp.int32(IDLE)
            for node, depth in DEPTH.items():
                lag = jnp.where(turned[tree] == node, LAGS[tick][depth], lag)
            lags.append(lag)
        deepest = jnp.maximum(jnp.maximum(lags[0], lags[1]), jnp.maximum(lags[2], lags[3]))
        deepest = jnp.where(me == tick, LEAST[tick], jnp.maximum(deepest, LEAST[tick]))
        return result, lags, deepest

    places = [place(tick) for tick in range(TICKS)]

    def chunk_copy(tick, block, tree, way):
        chunk = panel.at[tick, block, pl.ds(tree * CHUNK, CHUNK)]
        return pltpu.make_async_remote_copy(
            src_ref=chunk,
            dst_ref=chunk,
            send_sem=send_sem.at[tick, way],
            recv_sem=recv_sem.at[tick, block, tree],
            device_id={"blk": around[way]},
            device_id_type=pl.DeviceIdType.MESH,
        )

    def send(tick, block, tree):
        for way in range(4):
            @pl.when(places[tick][0][tree][way])
            def _():
                chunk_copy(tick, block, tree, way).start()

    def forward(tick, slot):
        for tree in range(4):
            index = slot - places[tick][1][tree]

            @pl.when((index >= 0) & (index < number(tick)))
            def _():
                block = tick + 1 + index
                chunk_copy(tick, block, tree, 0).wait_recv()
                send(tick, block, tree)

    def wait_load(block):
        pltpu.make_async_copy(front.at[pl.ds(0, BLOCK)], rows.at[block], load_sem.at[block]).wait()

    def invert(tick):
        matrix = rows[tick, :, :P_SIZE]
        line = lax.broadcasted_iota(jnp.int32, (P_SIZE, P_SIZE), 0)
        column = lax.broadcasted_iota(jnp.int32, (P_SIZE, P_SIZE), 1)
        eye = line == column
        on_diagonal = jnp.where(eye, matrix, 0.0)
        by_row = 1.0 / jnp.sum(on_diagonal, axis=1, keepdims=True)
        by_column = 1.0 / jnp.sum(on_diagonal, axis=0, keepdims=True)
        once = jnp.where(eye, 0.0, matrix * by_column)
        side = left(once)
        twice = dot(side, right(once))
        thrice = dot(side, right(twice))
        inverse[...] = right(by_row * (jnp.where(eye, 1.0, 0.0) - once + twice - thrice))

    def multiply(tick, block):
        mult = dot(left(rows[block, :, :P_SIZE]), inverse[...])
        rows[block, :, :P_SIZE] = mult
        panel[tick, block] = mult.astype(BF16)

    def pivot_rows(tick):
        keep = jnp.where(me > tick, 1.0, 0.0).astype(F32)
        urows[tick, :, :P_SIZE] = (rows[tick, :, :P_SIZE] * keep).astype(BF16)
        urows[tick, :, P_SIZE:] = rows[tick, :, P_SIZE:].astype(BF16)

    def loop(first, last, body):
        def step(index, carry):
            body(index)
            return carry

        lax.fori_loop(first, last, step, 0)

    wait_load(0)
    for block in range(1, BLOCKS):
        load(block)

    @pl.when(me == 0)
    def _():
        invert(0)

    pl.semaphore_wait(barrier, 4 + GROUPS - 1)

    @pl.when(me == 0)
    def _():
        def own(block):
            wait_load(block)
            multiply(0, block)
            for tree in range(4):
                send(0, block, tree)

        loop(1, BLOCKS, own)

    def slot_copy(offset):
        peer = lax.rem(mine + offset, GROUPS)
        return pltpu.make_async_remote_copy(
            src_ref=picked.at[peer],
            dst_ref=arrived.at[mine],
            send_sem=slot_send.at[offset],
            recv_sem=slot_recv.at[offset],
            device_id={"front": peer},
            device_id_type=pl.DeviceIdType.MESH,
        )

    def tag_copy(offset):
        peer = lax.rem(mine + offset, GROUPS)
        return pltpu.make_async_remote_copy(
            src_ref=labels.at[peer],
            dst_ref=tags.at[mine],
            send_sem=tag_send.at[offset],
            recv_sem=tag_recv.at[offset],
            device_id={"front": peer},
            device_id_type=pl.DeviceIdType.MESH,
        )

    slots = []
    for block in range(NB):
        slot = jnp.int32(0)
        for before in range(block):
            slot = slot + jnp.where(dest[before] == dest[block], 1, 0)
        slots.append(slot)
    lane = lax.broadcasted_iota(jnp.int32, (1, 128), 1)
    for group in range(GROUPS):
        label = jnp.full((1, 128), -1, jnp.int32)
        for block in range(NB):
            label = jnp.where(lane == jnp.where(dest[block] == group, slots[block], -1), target[block], label)
        labels[group] = label
    tags[mine] = labels[mine]
    for offset in range(1, GROUPS):
        tag_copy(offset).start()

    def exchange():
        keep = jnp.where(me >= TICKS, 1.0, 0.0).astype(F32)
        for block in range(NB):
            part = pl.ds(block % 2 * RB, RB)
            cont[block, :, :P_SIZE] = (rows[TICKS + block // 2, part, :P_SIZE] * keep).astype(BF16)
            cont[block, :, P_SIZE:] = rows[TICKS + block // 2, part, P_SIZE:].astype(BF16)
        cont[NB] = jnp.zeros((RB, WIDTH), BF16)
        for group in range(GROUPS):
            for slot in range(CAP):
                number_of = jnp.int32(NB)
                for block in range(NB):
                    number_of = jnp.where((dest[block] == group) & (slots[block] == slot), block, number_of)
                picked[group, slot] = cont[number_of]
        for offset in (4, 3, 5, 2, 6, 1, 7):
            slot_copy(offset).start()
        arrived[mine] = picked[mine]

    def update(tick, index, first):
        @pl.when((index >= 0) & (index < number(tick)))
        def _():
            block = tick + 1 + index
            if first:
                @pl.when(index == 0)
                def _():
                    pivot_rows(tick)

            if tick == 0:
                @pl.when(me != 0)
                def _():
                    wait_load(block)

            rows[block] = rows[block] - dot(panel[tick, block], urows[tick])
            if tick + 1 < TICKS:
                @pl.when(me == tick + 1)
                def _():
                    if first:
                        @pl.when(index == 0)
                        def _():
                            invert(tick + 1)

                    @pl.when(index > 0)
                    def _():
                        multiply(tick + 1, block)
                        for tree in range(4):
                            send(tick + 1, block, tree)
            elif first:
                @pl.when(block == TAIL)
                def _():
                    exchange()

    moves = [(FIRST_SLOT[tick] + LAGS[tick][1], FIRST_SLOT[tick] + number(tick) + LAGS[tick][5]) for tick in range(TICKS)]
    works = [(FIRST_SLOT[tick] + min(UPDATES[tick]), FIRST_SLOT[tick] + number(tick) + max(UPDATES[tick])) for tick in range(TICKS)]
    firsts = [FIRST_SLOT[tick] + max(UPDATES[tick]) + 3 for tick in range(TICKS)]
    marks = sorted({mark for pair in moves + works for mark in pair} | set(firsts))
    for begin, end in zip(marks[:-1], marks[1:]):
        def step(slot):
            for tick in range(TICKS):
                if moves[tick][0] <= begin < moves[tick][1]:
                    forward(tick, slot - FIRST_SLOT[tick])
            for tick in range(TICKS):
                if works[tick][0] <= begin < works[tick][1]:
                    update(tick, slot - FIRST_SLOT[tick] - places[tick][2], begin < firsts[tick])

        loop(begin, end, step)

    for offset in range(1, GROUPS):
        slot_copy(offset).wait()
        tag_copy(offset).wait()
    for tick in range(TICKS):
        for way in range(4):
            used = places[tick][0][0][way]
            for tree in range(1, 4):
                used = used | places[tick][0][tree][way]

            @pl.when(used)
            def _():
                sent = panel.at[tick, pl.ds(0, number(tick)), pl.ds(0, CHUNK)]
                pltpu.make_async_remote_copy(
                    src_ref=sent,
                    dst_ref=sent,
                    send_sem=send_sem.at[tick, way],
                    recv_sem=recv_sem.at[tick, 0, 0],
                    device_id={"blk": around[way]},
                    device_id_type=pl.DeviceIdType.MESH,
                ).wait_send()


def factor(front, dest, target):
    return pl.pallas_call(
        kernel,
        out_shape=(
            pltpu.VMEM((BLOCKS, BLOCK, WIDTH), F32),
            pltpu.VMEM((GROUPS, CAP, RB, WIDTH), BF16),
            pltpu.VMEM((GROUPS, 1, 128), jnp.int32),
        ),
        in_specs=[
            pl.BlockSpec(memory_space=pl.ANY),
            pl.BlockSpec(memory_space=pltpu.SMEM),
            pl.BlockSpec(memory_space=pltpu.SMEM),
        ],
        out_specs=(
            pl.BlockSpec(memory_space=pltpu.VMEM),
            pl.BlockSpec(memory_space=pltpu.VMEM),
            pl.BlockSpec(memory_space=pltpu.VMEM),
        ),
        scratch_shapes=[
            pltpu.VMEM((TICKS, BLOCKS, BLOCK, P_SIZE), BF16),
            pltpu.VMEM((TICKS, P_SIZE, WIDTH), BF16),
            pltpu.VMEM((3 * P_SIZE, P_SIZE), BF16),
            pltpu.VMEM((NB + 1, RB, WIDTH), BF16),
            pltpu.VMEM((GROUPS, CAP, RB, WIDTH), BF16),
            pltpu.VMEM((GROUPS, 1, 128), jnp.int32),
            pltpu.SemaphoreType.DMA((BLOCKS,)),
            pltpu.SemaphoreType.DMA((TICKS, 4)),
            pltpu.SemaphoreType.DMA((TICKS, BLOCKS, 4)),
            pltpu.SemaphoreType.DMA((GROUPS,)),
            pltpu.SemaphoreType.DMA((GROUPS,)),
            pltpu.SemaphoreType.DMA((GROUPS,)),
            pltpu.SemaphoreType.DMA((GROUPS,)),
        ],
        compiler_params=pltpu.CompilerParams(
            collective_id=0, has_side_effects=True, vmem_limit_bytes=45 * 1024 * 1024
        ),
        name="factor",
    )(front, dest, target)


def finish_kernel(
    rows, arrived, tags, base, factored, assembled, labels, tags_sem, total, rows_sem, base_sem, out_sem
):
    read = pltpu.make_async_copy(tags, labels, tags_sem)
    read.start()
    load = pltpu.make_async_copy(base, total, base_sem)
    load.start()
    copies = []
    for block in range(BLOCKS):
        at = 0
        for start, size in pieces(block):
            copies.append(
                pltpu.make_async_copy(
                    rows.at[block, pl.ds(at, size)], factored.at[pl.ds(start, size)], rows_sem.at[len(copies)]
                )
            )
            copies[-1].start()
            at += size
    load.wait()
    read.wait()
    for group in range(GROUPS):
        for slot in range(CAP):
            place = labels[group, 0, slot]

            @pl.when(place >= 0)
            def _():
                part = pl.ds(pl.multiple_of(place * RB, RB), RB)
                total[part] = total[part] + arrived[group, slot].astype(F32)

    store = pltpu.make_async_copy(total, assembled, out_sem)
    store.start()
    for copy in copies:
        copy.wait()
    store.wait()


def finish(rows, arrived, tags, base, shape):
    return pl.pallas_call(
        finish_kernel,
        out_shape=(jax.ShapeDtypeStruct(shape, F32), jax.ShapeDtypeStruct(base.shape, F32)),
        in_specs=[
            pl.BlockSpec(memory_space=pltpu.VMEM),
            pl.BlockSpec(memory_space=pltpu.VMEM),
            pl.BlockSpec(memory_space=pltpu.VMEM),
            pl.BlockSpec(memory_space=pl.ANY),
        ],
        out_specs=(pl.BlockSpec(memory_space=pl.ANY), pl.BlockSpec(memory_space=pl.ANY)),
        scratch_shapes=[
            pltpu.SMEM((GROUPS, 1, 128), jnp.int32),
            pltpu.SemaphoreType.DMA,
            pltpu.VMEM((ASM_BLOCKS * RB, WIDTH), F32),
            pltpu.SemaphoreType.DMA((BLOCKS + 2,)),
            pltpu.SemaphoreType.DMA,
            pltpu.SemaphoreType.DMA,
        ],
        compiler_params=pltpu.CompilerParams(vmem_limit_bytes=16 * 1024 * 1024),
        name="finish",
    )(rows, arrived, tags, base)


def local(front, parent_group, row_block, parent_base):
    rows, arrived, tags = factor(front, parent_group.reshape(NB), row_block.reshape(NB))
    return finish(rows, arrived, tags, parent_base, front.shape)


def solution(mesh):
    placed = (
        P("front", "blk"),
        P("front", "blk", None, None),
        P("front", "blk", None),
        P("front", "blk"),
    )
    return jax.shard_map(
        local,
        mesh=mesh,
        in_specs=placed,
        out_specs=(P("front", "blk"), P("front", "blk")),
        check_vma=False,
    )
```

```python
import jax
import jax.numpy as jnp
from jax import lax
from jax.experimental import pallas as pl
from jax.experimental.pallas import tpu as pltpu
from jax.sharding import PartitionSpec as P

P_SIZE = 256
TICKS = 5
RB = 128
NB = 6
CAP = 2
ASM_BLOCKS = 8
GROUPS = 8
SIDE = 4
WIDTH = 384
BLOCK = 256
HALF = BLOCK // 2
CHUNK = BLOCK // 4
LAGS = (
    (0, 2, 8, 13, 22, 28),
    (0, 5, 6, 15, 20, 26),
    (0, 2, 9, 16, 21, 34),
    (0, 1, 8, 12, 15, 30),
    (0, 1, 4, 12, 13, 19),
)
FIRST_SLOT = (0, 28, 43, 66, 85)
LEAST = (22, 3, 10, 15, 3)
IDLE = 1000
UPDATES = tuple(tuple(max(LEAST[tick], LAGS[tick][depth]) for depth in (0, 3, 4, 5)) for tick in range(TICKS))
TAIL = 7
BLOCKS = 24
F32 = jnp.float32
BF16 = jnp.bfloat16

STEPS = ((1, 0), (0, 1), (-1, 0), (0, -1))
PARENT = {
    (1, 0): 0, (2, 0): 0, (3, 0): 0, (0, 1): 2, (1, 1): 1, (2, 1): 0, (3, 1): 0, (0, 2): 2,
    (1, 2): 1, (2, 2): 1, (3, 2): 0, (0, 3): 2, (1, 3): 3, (2, 3): 3, (3, 3): 0,
}
SENDERS = tuple(
    sorted(
        ((x - STEPS[way][0]) % SIDE) + SIDE * ((z - STEPS[way][1]) % SIDE)
        for (x, z), own in PARENT.items()
        if own == way
    )
    for way in range(4)
)


def depth_of(node):
    depth = 0
    while node != (0, 0):
        step = STEPS[PARENT[node]]
        node = ((node[0] - step[0]) % SIDE, (node[1] - step[1]) % SIDE)
        depth += 1
    return depth


DEPTH = {x + SIDE * z: depth_of((x, z)) for x, z in PARENT}


def pieces(block):
    if block < TICKS:
        return ((block * WIDTH, BLOCK),)
    if block < 8:
        return ((5376 + (block - TICKS) * BLOCK, BLOCK),)
    if block < 10:
        first = (block - 8) * 2 * WIDTH + P_SIZE
        return ((first, HALF), (first + WIDTH, HALF))
    return ((1792 + (block - 10) * BLOCK, BLOCK),)


def number(tick):
    return BLOCKS - 1 - tick


def split(value):
    high = value.astype(BF16)
    return high, (value - high.astype(F32)).astype(BF16)


def dot(a, b):
    return jnp.dot(a, b, preferred_element_type=F32)


def left(value):
    high, low = split(value)
    return jnp.concatenate([high, high, low], axis=1)


def right(value):
    high, low = split(value)
    return jnp.concatenate([high, low, high], axis=0)


def kernel(
    front, dest, target, rows, arrived, tags, panel, urows, inverse, cont, picked, labels,
    load_sem, send_sem, recv_sem, slot_send, slot_recv, tag_send, tag_recv,
):
    me = lax.axis_index("blk")
    mine = lax.axis_index("front")
    x = lax.rem(me, SIDE)
    z = lax.div(me, SIDE)
    around = [
        z * SIDE + lax.rem(x + 1, SIDE),
        lax.rem(z + 1, SIDE) * SIDE + x,
        z * SIDE + lax.rem(x + SIDE - 1, SIDE),
        lax.rem(z + SIDE - 1, SIDE) * SIDE + x,
    ]

    barrier = pltpu.get_barrier_semaphore()
    for other in around:
        pl.semaphore_signal(barrier, inc=1, device_id={"blk": other}, device_id_type=pl.DeviceIdType.MESH)
    for offset in range(1, GROUPS):
        pl.semaphore_signal(
            barrier,
            inc=1,
            device_id={"front": lax.rem(mine + offset, GROUPS)},
            device_id_type=pl.DeviceIdType.MESH,
        )

    def load(block):
        at = 0
        for start, size in pieces(block):
            pltpu.make_async_copy(
                front.at[pl.ds(start, size)], rows.at[block, pl.ds(at, size)], load_sem.at[block]
            ).start()
            at += size

    load(0)

    def place(tick):
        dx = lax.rem(x - tick % SIDE + SIDE, SIDE)
        dz = lax.rem(z - tick // SIDE + SIDE, SIDE)
        nx, nz = lax.rem(SIDE - dx, SIDE), lax.rem(SIDE - dz, SIDE)
        turned = (dx + SIDE * dz, dz + SIDE * nx, nx + SIDE * nz, nz + SIDE * dx)
        result = []
        lags = []
        for tree in range(4):
            ways = []
            for way in range(4):
                has = turned[tree] == SENDERS[(way - tree) % 4][0]
                for node in SENDERS[(way - tree) % 4][1:]:
                    has = has | (turned[tree] == node)
                ways.append(has)
            result.append(ways)
            lag = jnp.int32(IDLE)
            for node, depth in DEPTH.items():
                lag = jnp.where(turned[tree] == node, LAGS[tick][depth], lag)
            lags.append(lag)
        deepest = jnp.maximum(jnp.maximum(lags[0], lags[1]), jnp.maximum(lags[2], lags[3]))
        deepest = jnp.where(me == tick, LEAST[tick], jnp.maximum(deepest, LEAST[tick]))
        return result, lags, deepest

    places = [place(tick) for tick in range(TICKS)]

    def chunk_copy(tick, block, tree, way):
        chunk = panel.at[tick, block, pl.ds(tree * CHUNK, CHUNK)]
        return pltpu.make_async_remote_copy(
            src_ref=chunk,
            dst_ref=chunk,
            send_sem=send_sem.at[tick, way],
            recv_sem=recv_sem.at[tick, block, tree],
            device_id={"blk": around[way]},
            device_id_type=pl.DeviceIdType.MESH,
        )

    def send(tick, block, tree):
        for way in range(4):
            @pl.when(places[tick][0][tree][way])
            def _():
                chunk_copy(tick, block, tree, way).start()

    def forward(tick, slot):
        for tree in range(4):
            index = slot - places[tick][1][tree]

            @pl.when((index >= 0) & (index < number(tick)))
            def _():
                block = tick + 1 + index
                chunk_copy(tick, block, tree, 0).wait_recv()
                send(tick, block, tree)

    def wait_load(block):
        pltpu.make_async_copy(front.at[pl.ds(0, BLOCK)], rows.at[block], load_sem.at[block]).wait()

    def invert(tick):
        matrix = rows[tick, :, :P_SIZE]
        line = lax.broadcasted_iota(jnp.int32, (P_SIZE, P_SIZE), 0)
        column = lax.broadcasted_iota(jnp.int32, (P_SIZE, P_SIZE), 1)
        eye = line == column
        on_diagonal = jnp.where(eye, matrix, 0.0)
        by_row = 1.0 / jnp.sum(on_diagonal, axis=1, keepdims=True)
        by_column = 1.0 / jnp.sum(on_diagonal, axis=0, keepdims=True)
        once = jnp.where(eye, 0.0, matrix * by_column)
        side = left(once)
        twice = dot(side, right(once))
        thrice = dot(side, right(twice))
        inverse[...] = right(by_row * (jnp.where(eye, 1.0, 0.0) - once + twice - thrice))

    def multiply(tick, block):
        mult = dot(left(rows[block, :, :P_SIZE]), inverse[...])
        rows[block, :, :P_SIZE] = mult
        panel[tick, block] = mult.astype(BF16)

    def pivot_rows(tick):
        keep = jnp.where(me > tick, 1.0, 0.0).astype(F32)
        urows[tick, :, :P_SIZE] = (rows[tick, :, :P_SIZE] * keep).astype(BF16)
        urows[tick, :, P_SIZE:] = rows[tick, :, P_SIZE:].astype(BF16)

    def loop(first, last, body):
        def step(index, carry):
            body(index)
            return carry

        lax.fori_loop(first, last, step, 0)

    wait_load(0)
    for block in range(1, BLOCKS):
        load(block)

    @pl.when(me == 0)
    def _():
        invert(0)

    pl.semaphore_wait(barrier, 4 + GROUPS - 1)

    @pl.when(me == 0)
    def _():
        def own(block):
            wait_load(block)
            multiply(0, block)
            for tree in range(4):
                send(0, block, tree)

        loop(1, BLOCKS, own)

    pivot_rows(0)

    def slot_copy(offset):
        peer = lax.rem(mine + offset, GROUPS)
        return pltpu.make_async_remote_copy(
            src_ref=picked.at[peer],
            dst_ref=arrived.at[mine],
            send_sem=slot_send.at[offset],
            recv_sem=slot_recv.at[offset],
            device_id={"front": peer},
            device_id_type=pl.DeviceIdType.MESH,
        )

    def tag_copy(offset):
        peer = lax.rem(mine + offset, GROUPS)
        return pltpu.make_async_remote_copy(
            src_ref=labels.at[peer],
            dst_ref=tags.at[mine],
            send_sem=tag_send.at[offset],
            recv_sem=tag_recv.at[offset],
            device_id={"front": peer},
            device_id_type=pl.DeviceIdType.MESH,
        )

    slots = []
    for block in range(NB):
        slot = jnp.int32(0)
        for before in range(block):
            slot = slot + jnp.where(dest[before] == dest[block], 1, 0)
        slots.append(slot)
    lane = lax.broadcasted_iota(jnp.int32, (1, 128), 1)
    for group in range(GROUPS):
        label = jnp.full((1, 128), -1, jnp.int32)
        for block in range(NB):
            label = jnp.where(lane == jnp.where(dest[block] == group, slots[block], -1), target[block], label)
        labels[group] = label
    tags[mine] = labels[mine]
    for offset in range(1, GROUPS):
        tag_copy(offset).start()

    def exchange():
        keep = jnp.where(me >= TICKS, 1.0, 0.0).astype(F32)
        for block in range(NB):
            part = pl.ds(block % 2 * RB, RB)
            cont[block, :, :P_SIZE] = (rows[TICKS + block // 2, part, :P_SIZE] * keep).astype(BF16)
            cont[block, :, P_SIZE:] = rows[TICKS + block // 2, part, P_SIZE:].astype(BF16)
        cont[NB] = jnp.zeros((RB, WIDTH), BF16)
        for offset in (4, 3, 5, 2, 6, 1, 7, 0):
            group = lax.rem(mine + offset, GROUPS)
            for slot in range(CAP):
                number_of = jnp.int32(NB)
                for block in range(NB):
                    number_of = jnp.where((dest[block] == group) & (slots[block] == slot), block, number_of)
                picked[group, slot] = cont[number_of]
            if offset:
                slot_copy(offset).start()
        arrived[mine] = picked[mine]

    def update(tick, index, first):
        @pl.when((index >= 0) & (index < number(tick)))
        def _():
            block = tick + 1 + index
            if tick == 0:
                @pl.when(me != 0)
                def _():
                    wait_load(block)

            rows[block] = rows[block] - dot(panel[tick, block], urows[tick])
            if tick + 1 < TICKS:
                @pl.when(me == tick + 1)
                def _():
                    if first:
                        @pl.when(index == 0)
                        def _():
                            invert(tick + 1)

                    @pl.when(index > 0)
                    def _():
                        multiply(tick + 1, block)
                        for tree in range(4):
                            send(tick + 1, block, tree)

                if first:
                    @pl.when(index == 0)
                    def _():
                        pivot_rows(tick + 1)

            elif first:
                @pl.when(block == TAIL)
                def _():
                    exchange()

    moves = [(FIRST_SLOT[tick] + LAGS[tick][1], FIRST_SLOT[tick] + number(tick) + LAGS[tick][5]) for tick in range(TICKS)]
    works = [(FIRST_SLOT[tick] + min(UPDATES[tick]), FIRST_SLOT[tick] + number(tick) + max(UPDATES[tick])) for tick in range(TICKS)]
    firsts = [FIRST_SLOT[tick] + max(UPDATES[tick]) + 3 for tick in range(TICKS)]
    marks = sorted({mark for pair in moves + works for mark in pair} | set(firsts))
    for begin, end in zip(marks[:-1], marks[1:]):
        def step(slot):
            for tick in range(TICKS):
                if moves[tick][0] <= begin < moves[tick][1]:
                    forward(tick, slot - FIRST_SLOT[tick])
            for tick in range(TICKS):
                if works[tick][0] <= begin < works[tick][1]:
                    update(tick, slot - FIRST_SLOT[tick] - places[tick][2], begin < firsts[tick])

        loop(begin, end, step)

    for offset in range(1, GROUPS):
        slot_copy(offset).wait()
        tag_copy(offset).wait()
    for tick in range(TICKS):
        for way in range(4):
            used = places[tick][0][0][way]
            for tree in range(1, 4):
                used = used | places[tick][0][tree][way]

            @pl.when(used)
            def _():
                sent = panel.at[tick, pl.ds(0, number(tick)), pl.ds(0, CHUNK)]
                pltpu.make_async_remote_copy(
                    src_ref=sent,
                    dst_ref=sent,
                    send_sem=send_sem.at[tick, way],
                    recv_sem=recv_sem.at[tick, 0, 0],
                    device_id={"blk": around[way]},
                    device_id_type=pl.DeviceIdType.MESH,
                ).wait_send()


def factor(front, dest, target):
    return pl.pallas_call(
        kernel,
        out_shape=(
            pltpu.VMEM((BLOCKS, BLOCK, WIDTH), F32),
            pltpu.VMEM((GROUPS, CAP, RB, WIDTH), BF16),
            pltpu.VMEM((GROUPS, 1, 128), jnp.int32),
        ),
        in_specs=[
            pl.BlockSpec(memory_space=pl.ANY),
            pl.BlockSpec(memory_space=pltpu.SMEM),
            pl.BlockSpec(memory_space=pltpu.SMEM),
        ],
        out_specs=(
            pl.BlockSpec(memory_space=pltpu.VMEM),
            pl.BlockSpec(memory_space=pltpu.VMEM),
            pl.BlockSpec(memory_space=pltpu.VMEM),
        ),
        scratch_shapes=[
            pltpu.VMEM((TICKS, BLOCKS, BLOCK, P_SIZE), BF16),
            pltpu.VMEM((TICKS, P_SIZE, WIDTH), BF16),
            pltpu.VMEM((3 * P_SIZE, P_SIZE), BF16),
            pltpu.VMEM((NB + 1, RB, WIDTH), BF16),
            pltpu.VMEM((GROUPS, CAP, RB, WIDTH), BF16),
            pltpu.VMEM((GROUPS, 1, 128), jnp.int32),
            pltpu.SemaphoreType.DMA((BLOCKS,)),
            pltpu.SemaphoreType.DMA((TICKS, 4)),
            pltpu.SemaphoreType.DMA((TICKS, BLOCKS, 4)),
            pltpu.SemaphoreType.DMA((GROUPS,)),
            pltpu.SemaphoreType.DMA((GROUPS,)),
            pltpu.SemaphoreType.DMA((GROUPS,)),
            pltpu.SemaphoreType.DMA((GROUPS,)),
        ],
        compiler_params=pltpu.CompilerParams(
            collective_id=0, has_side_effects=True, vmem_limit_bytes=45 * 1024 * 1024
        ),
        name="factor",
    )(front, dest, target)


def finish_kernel(
    rows, arrived, tags, base, factored, assembled, labels, tags_sem, total, rows_sem, base_sem, out_sem
):
    read = pltpu.make_async_copy(tags, labels, tags_sem)
    read.start()
    load = pltpu.make_async_copy(base, total, base_sem)
    load.start()
    copies = []
    for block in range(BLOCKS):
        at = 0
        for start, size in pieces(block):
            copies.append(
                pltpu.make_async_copy(
                    rows.at[block, pl.ds(at, size)], factored.at[pl.ds(start, size)], rows_sem.at[len(copies)]
                )
            )
            copies[-1].start()
            at += size
    load.wait()
    read.wait()
    for group in range(GROUPS):
        for slot in range(CAP):
            place = labels[group, 0, slot]

            @pl.when(place >= 0)
            def _():
                part = pl.ds(pl.multiple_of(place * RB, RB), RB)
                total[part] = total[part] + arrived[group, slot].astype(F32)

    store = pltpu.make_async_copy(total, assembled, out_sem)
    store.start()
    for copy in copies:
        copy.wait()
    store.wait()


def finish(rows, arrived, tags, base, shape):
    return pl.pallas_call(
        finish_kernel,
        out_shape=(jax.ShapeDtypeStruct(shape, F32), jax.ShapeDtypeStruct(base.shape, F32)),
        in_specs=[
            pl.BlockSpec(memory_space=pltpu.VMEM),
            pl.BlockSpec(memory_space=pltpu.VMEM),
            pl.BlockSpec(memory_space=pltpu.VMEM),
            pl.BlockSpec(memory_space=pl.ANY),
        ],
        out_specs=(pl.BlockSpec(memory_space=pl.ANY), pl.BlockSpec(memory_space=pl.ANY)),
        scratch_shapes=[
            pltpu.SMEM((GROUPS, 1, 128), jnp.int32),
            pltpu.SemaphoreType.DMA,
            pltpu.VMEM((ASM_BLOCKS * RB, WIDTH), F32),
            pltpu.SemaphoreType.DMA((BLOCKS + 2,)),
            pltpu.SemaphoreType.DMA,
            pltpu.SemaphoreType.DMA,
        ],
        compiler_params=pltpu.CompilerParams(vmem_limit_bytes=16 * 1024 * 1024),
        name="finish",
    )(rows, arrived, tags, base)


def local(front, parent_group, row_block, parent_base):
    rows, arrived, tags = factor(front, parent_group.reshape(NB), row_block.reshape(NB))
    return finish(rows, arrived, tags, parent_base, front.shape)


def solution(mesh):
    placed = (
        P("front", "blk"),
        P("front", "blk", None, None),
        P("front", "blk", None),
        P("front", "blk"),
    )
    return jax.shard_map(
        local,
        mesh=mesh,
        in_specs=placed,
        out_specs=(P("front", "blk"), P("front", "blk")),
        check_vma=False,
    )
```
